32 devices in a mesh: slab: 8 (over z, y), band: 4 (over x, core).
Axes of the slice: x: 2, y: 2, z: 4, core: 2. Of those that a mesh axis runs over, the one named last changes fastest.
Arguments:
- orbitals: float32 [8, 128, 128, 128], P('band', 'slab'), may hold values from -6 to 6
Outputs:
- exchange_out: float32 [8, 128, 128, 128], P('band', 'slab')
The draws below stay inside these ranges and needn't reach their ends.
All inputs are finite; a program needn't handle non-finite values.
Results may differ from the reference program's by a relative error of at most 0.00013.
Values sent between devices are 32-bit elements; how exact they have to be, the bound alone decides.
No kernel may reach another device: no remote copies, remote signals or barrier semaphores. Data moves between devices by JAX's collectives and lax.ppermute only.
A program may use at most 64 MiB of HBM per device.

```python
import math
import jax
import jax.numpy as jnp
from jax import lax

NX = 128
NY = 128
NZ = 128
OB = 2
NORB = 8
N_BAND = 4


def block_levels(key, shape, cuts, low, high):
    level, own = 1.0, jax.random.fold_in(key, 6)
    for position, blocks in cuts:
        heights = jnp.exp(jax.random.uniform(jax.random.fold_in(own, position), (blocks,), jnp.float32, low / len(cuts), high / len(cuts)))
        level = level * jnp.repeat(heights, shape[position] // blocks).reshape([-1 if axis == position else 1 for axis in range(len(shape))])
    return level


def bell_draw(rng, dims, spread, limit, cuts=(), held_as=jnp.bfloat16):
    entries = jax.random.normal(rng, dims, jnp.float32) * spread
    if len(cuts) > 0:
        entries = block_levels(rng, dims, cuts, -0.22, 0.18) * entries
    return jnp.clip(entries, min=-limit, max=limit).astype(held_as)


def setup_inputs(seed: int = 0) -> dict:
    key_list = jax.random.split(jax.random.key(seed), 2)
    orbitals = bell_draw(key_list[0], (NORB, NZ, NY, NX), 1.0, 6.0, ((0, 4), (1, 8)), jnp.float32)
    return dict(orbitals=orbitals)


screen_width = 0.5


def frequency(counter, length):
    return jnp.where(counter < length // 2, counter, counter - length).astype(jnp.float32)


def screened(squared):
    safe_sq = jnp.where(squared > 0, squared, 1.0)
    value = 4.0 * math.pi / safe_sq * (1.0 - jnp.exp(-safe_sq / (4.0 * screen_width ** 2)))
    return jnp.where(squared > 0, value, math.pi / screen_width ** 2)


def kernel_half():
    freq_z = frequency(jnp.arange(NZ, dtype=jnp.int32), NZ)
    freq_y = frequency(jnp.arange(NY, dtype=jnp.int32), NY)
    freq_x = jnp.arange(NX // 2 + 1, dtype=jnp.int32).astype(jnp.float32)
    squared = ((2.0 * math.pi / NZ) * freq_z) ** 2
    squared = squared[:, None, None] + (((2.0 * math.pi / NY) * freq_y) ** 2)[None, :, None]
    squared = squared + (((2.0 * math.pi / NX) * freq_x) ** 2)[None, None, :]
    return screened(squared)


def reference(orbitals):
    blocks = orbitals.reshape(N_BAND, OB, NZ, NY, NX)
    partner = jnp.roll(blocks, 1, axis=0)
    weights = kernel_half()

    def one_block(pair_args):
        own_block, other_block = pair_args
        partners = jnp.concatenate([own_block, other_block], axis=0)

        def one_target(target):
            def add_term(accum, partner_orb):
                density = target * partner_orb
                spectrum = jnp.fft.rfftn(density, axes=(0, 1, 2))
                potential = jnp.fft.irfftn(weights * spectrum, s=(NZ, NY, NX), axes=(0, 1, 2))
                return accum + potential * partner_orb, None

            accum, unused = lax.scan(add_term, jnp.zeros_like(target), partners)
            return -accum

        return lax.map(one_target, own_block)

    result = lax.map(one_block, (blocks, partner))
    return result.reshape(NORB, NZ, NY, NX)
```

```python
import functools
import math

import jax
import jax.numpy as jnp
from jax import lax
from jax.experimental import pallas as pl
from jax.experimental.pallas import tpu as pltpu
from jax.sharding import Mesh, PartitionSpec as P

screen_width = 0.5
highest = lax.Precision.HIGHEST


def frequency(counter, length):
    return jnp.where(counter < length // 2, counter, counter - length).astype(jnp.float32)


def screened(squared):
    safe_sq = jnp.where(squared > 0, squared, 1.0)
    value = 4.0 * math.pi / safe_sq * (1.0 - jnp.exp(-safe_sq / (4.0 * screen_width**2)))
    return jnp.where(squared > 0, value, math.pi / screen_width**2)


def cas_table(rows, columns, length):
    product = rows[:, None] * columns[None, :] % length
    angles = 2.0 * math.pi / length * product.astype(jnp.float32)
    return jnp.cos(angles) + jnp.sin(angles)


def halves(value):
    high = value.astype(jnp.bfloat16)
    return high, (value - high.astype(jnp.float32)).astype(jnp.bfloat16)


def table_halves(table):
    high = lax.reduce_precision(table, exponent_bits=8, mantissa_bits=7)
    return high.astype(jnp.bfloat16), (table - high).astype(jnp.bfloat16)


def right_table(table):
    high, low = table_halves(table)
    top = jnp.concatenate([high, low], axis=1)
    return jnp.concatenate([top, jnp.concatenate([high, jnp.zeros_like(low)], axis=1)], axis=0)


def left_table(table):
    high, low = table_halves(table)
    top = jnp.concatenate([high, high], axis=1)
    return jnp.concatenate([top, jnp.concatenate([low, jnp.zeros_like(low)], axis=1)], axis=0)


def times_right(value, table):
    width = value.shape[1]
    high, low = halves(value)
    both = jnp.dot(
        jnp.concatenate([high, low], axis=1), table, preferred_element_type=jnp.float32
    )
    return both[:, :width] + both[:, width:]


def times_left(table, value):
    high, low = halves(value)
    both = jnp.dot(
        table, jnp.concatenate([high, low], axis=0), preferred_element_type=jnp.float32
    )
    rows = both.shape[0] // 2
    return both[:rows] + both[rows:]


def forward_kernel(group, left_ref, right_ref, first_ref, second_ref, out_ref):
    planes, rows, columns = first_ref.shape[-3:]
    share = rows // group
    for plane in range(0, planes, 2):
        density = first_ref[0, plane : plane + 2] * second_ref[0, plane : plane + 2]
        part = times_right(density.reshape(2 * rows, columns), right_ref[...])
        part = times_left(left_ref[...], jnp.concatenate([part[:rows], part[rows:]], axis=1))
        for offset in range(2):
            piece = part[:, offset * columns : (offset + 1) * columns]
            for chunk in range(group):
                out_ref[chunk, 0, pl.ds(plane + offset, share, stride=planes), :] = piece[
                    chunk * share : (chunk + 1) * share
                ]


def depth_kernel(planes, forth_ref, back_ref, weight_ref, in_ref, out_ref):
    group = in_ref.shape[0]
    share = in_ref.shape[2] // planes
    columns = in_ref.shape[3]
    for row in range(0, share, 2):
        value = jnp.concatenate(
            [
                jnp.concatenate(
                    [
                        in_ref[chunk, 0, (row + offset) * planes : (row + offset + 1) * planes, :]
                        for chunk in range(group)
                    ],
                    axis=0,
                )
                for offset in range(2)
            ],
            axis=1,
        )
        value = times_left(forth_ref[...], value) * weight_ref[row // 2]
        value = times_left(back_ref[...], value)
        for offset in range(2):
            for chunk in range(group):
                out_ref[chunk, 0, (row + offset) * planes : (row + offset + 1) * planes, :] = value[
                    chunk * planes : (chunk + 1) * planes,
                    offset * columns : (offset + 1) * columns,
                ]


def potential_planes(plane, planes, left_ref, right_ref, in_ref):
    group = in_ref.shape[0]
    share = in_ref.shape[2] // planes
    value = jnp.concatenate(
        [
            jnp.concatenate(
                [
                    in_ref[chunk, 0, pl.ds(plane + offset, share, stride=planes), :]
                    for chunk in range(group)
                ],
                axis=0,
            )
            for offset in range(2)
        ],
        axis=1,
    )
    columns = in_ref.shape[3]
    rows = group * share
    value = times_left(left_ref[...], value)
    value = jnp.concatenate([value[:, :columns], value[:, columns:]], axis=0)
    return times_right(value, right_ref[...]).reshape(2, rows, columns)


def inverse_kernel(uses, targets, left_ref, right_ref, in_ref, *refs):
    factors = {factor for _, factor, _ in uses}
    factor_refs = dict(zip(sorted(factors), refs[: len(factors)]))
    rest = refs[len(factors) :]
    held = [target for target, _, add in uses if add]
    held_refs = dict(zip(held, rest[: len(held)]))
    out_refs = dict(zip(targets, rest[len(held) :]))
    planes = rest[-1].shape[0]
    for plane in range(0, planes, 2):
        field = potential_planes(plane, planes, left_ref, right_ref, in_ref)
        for target, factor, add in uses:
            term = field * factor_refs[factor][0, plane : plane + 2]
            if add:
                out_refs[target][plane : plane + 2] = held_refs[target][plane : plane + 2] - term
            else:
                out_refs[target][plane : plane + 2] = -term


def whole(shape):
    return pl.BlockSpec(shape, lambda *grid: (0,) * len(shape))


def cost(steps):
    return pl.CostEstimate(flops=steps * 700_000_000, bytes_accessed=steps * 3_000_000, transcendentals=0)


def forward(first, second, first_of, second_of, count, group, left, right):
    planes, rows, columns = first.shape[1:]
    plane_block = (1, planes, rows, columns)
    return pl.pallas_call(
        functools.partial(forward_kernel, group),
        grid=(count,),
        in_specs=[
            whole(left.shape),
            whole(right.shape),
            pl.BlockSpec(plane_block, lambda step: (first_of(step), 0, 0, 0)),
            pl.BlockSpec(plane_block, lambda step: (second_of(step), 0, 0, 0)),
        ],
        out_specs=pl.BlockSpec(
            (group, 1, rows // group * planes, columns), lambda step: (0, step, 0, 0)
        ),
        out_shape=jax.ShapeDtypeStruct(
            (group, count, rows // group * planes, columns), jnp.float32
        ),
        cost_estimate=cost(count),
        name="forward",
    )(left, right, first, second)


def through_depth(value, planes, forth, back, weight):
    group, count, lines, columns = value.shape
    block = pl.BlockSpec((group, 1, lines, columns), lambda step: (0, step, 0, 0))
    return pl.pallas_call(
        functools.partial(depth_kernel, planes),
        grid=(count,),
        in_specs=[whole(forth.shape), whole(back.shape), whole(weight.shape), block],
        out_specs=block,
        out_shape=jax.ShapeDtypeStruct(value.shape, jnp.float32),
        cost_estimate=cost(count),
        name="through_depth",
    )(forth, back, weight, value)


def inverse(value, which, uses, orbital_sets, held, left, right):
    group, _, lines, columns = value.shape
    grid_shape = orbital_sets[0].shape[1:]
    described = [(target, factor, target in held) for target, factor in uses]
    factors = sorted({factor for _, factor in uses})
    targets = [target for target, _ in uses]
    plane_block = (1,) + grid_shape
    specs = [
        whole(left.shape),
        whole(right.shape),
        pl.BlockSpec((group, 1, lines, columns), lambda step: (0, which, 0, 0)),
    ]
    args = [left, right, value]
    for orbital_set, index in factors:
        specs.append(pl.BlockSpec(plane_block, lambda step, index=index: (index, 0, 0, 0)))
        args.append(orbital_sets[orbital_set])
    for target in targets:
        if target in held:
            specs.append(whole(grid_shape))
            args.append(held[target])
    results = pl.pallas_call(
        functools.partial(inverse_kernel, described, targets),
        grid=(1,),
        in_specs=specs,
        out_specs=[whole(grid_shape)] * len(targets),
        out_shape=[jax.ShapeDtypeStruct(grid_shape, jnp.float32)] * len(targets),
        cost_estimate=cost(1),
        name="inverse",
    )(*args)
    return {**held, **dict(zip(targets, results))}


def layered_body(orbitals):
    blocks = lax.axis_size("band")
    inner = lax.axis_size("inner")
    count, planes, rows, columns = orbitals.shape
    piece = planes // blocks
    group = inner * blocks
    depth = planes * inner * blocks
    share = rows // group

    moved = orbitals.reshape(count, blocks, piece, rows, columns)
    moved = lax.all_to_all(moved, "band", split_axis=1, concat_axis=1, tiled=True)
    moved = lax.all_to_all(moved, "layer", split_axis=1, concat_axis=1, tiled=True)
    own = moved.reshape(count, planes, rows, columns)
    pairs = [(source, (source + 1) % blocks) for source in range(blocks)]
    other = lax.ppermute(own, "layer", pairs)

    counter = jnp.arange(columns, dtype=jnp.int32)
    across = right_table(cas_table(counter, counter, columns))
    counter = jnp.arange(rows, dtype=jnp.int32)
    along = left_table(cas_table(counter, counter, rows))
    counter = jnp.arange(depth, dtype=jnp.int32)
    source, local = counter // planes, counter % planes
    place = local // piece * (inner * planes) + source // blocks * planes
    place = place + source % blocks * piece + local % piece
    forth_table = cas_table(counter, place, depth)
    forth = left_table(forth_table)
    back = left_table(forth_table.T)

    me = lax.axis_index(("inner", "band"))
    freq_z = 2.0 * math.pi / depth * frequency(counter, depth)
    mine = me * share + jnp.arange(share, dtype=jnp.int32)
    freq_y = 2.0 * math.pi / rows * frequency(mine, rows)
    freq_x = 2.0 * math.pi / columns * frequency(jnp.arange(columns, dtype=jnp.int32), columns)
    squared = (freq_y**2).reshape(share // 2, 1, 2, 1) + (freq_z**2)[None, :, None, None]
    squared = squared + (freq_x**2)[None, None, None, :]
    weight = screened(squared) * (1.0 / (columns * rows * depth))
    weight = weight.reshape(share // 2, depth, 2 * columns)

    def exchange(value):
        return lax.all_to_all(value, ("inner", "band"), split_axis=0, concat_axis=0, tiled=True)

    sets = (own, other)
    held = {}
    own_pairs = [(i, j) for i in range(count) for j in range(i, count)]
    batches = []
    for i, j in own_pairs:
        uses = [(i, (0, j))] + ([(j, (0, i))] if i != j else [])
        batches.append((own, own, lambda step, i=i: i, lambda step, j=j: j, 1, [uses]))
    for i in range(count):
        uses = [[(i, (1, j))] for j in range(count)]
        batches.append((own, other, lambda step, i=i: i, lambda step: step, count, uses))
    for first, second, first_of, second_of, number, uses in batches:
        value = forward(first, second, first_of, second_of, number, group, along, across)
        value = exchange(value)
        value = through_depth(value, planes, forth, back, weight)
        value = exchange(value)
        for which in range(number):
            held = inverse(value, which, uses[which], sets, held, along, across)

    out = jnp.stack([held[i] for i in range(count)])
    out = out.reshape(count, blocks, piece, rows, columns)
    out = lax.all_to_all(out, "layer", split_axis=1, concat_axis=1, tiled=True)
    out = lax.all_to_all(out, "band", split_axis=1, concat_axis=1, tiled=True)
    return out.reshape(count, planes, rows, columns)


def exchange_sum(value, split_axis, concat_axis):
    return lax.all_to_all(value, "slab", split_axis=split_axis, concat_axis=concat_axis, tiled=True)


def plain_body(orbitals):
    count, planes, rows, columns = orbitals.shape
    depth = planes * lax.axis_size("slab")
    blocks = lax.axis_size("band")
    pairs = [(source, (source + 1) % blocks) for source in range(blocks)]
    neighbour = lax.ppermute(orbitals, "band", pairs)
    x_count = jnp.arange(columns, dtype=jnp.int32)
    y_count = jnp.arange(rows, dtype=jnp.int32)
    z_count = jnp.arange(depth, dtype=jnp.int32)
    cas_x = cas_table(x_count, x_count, columns)
    cas_y = cas_table(y_count, y_count, rows)
    cas_z = cas_table(z_count, z_count, depth)
    slabs = lax.axis_size("slab")
    split_axis, extent = (2, rows) if rows % slabs == 0 else (3, columns)
    share = extent // slabs
    mine = lax.axis_index("slab") * share + jnp.arange(share, dtype=jnp.int32)
    y_rows, x_rows = (mine, x_count) if split_axis == 2 else (y_count, mine)
    squared = ((2.0 * math.pi / depth * frequency(z_count, depth)) ** 2)[:, None, None]
    squared = squared + ((2.0 * math.pi / rows * frequency(y_rows, rows)) ** 2)[None, :, None]
    squared = squared + ((2.0 * math.pi / columns * frequency(x_rows, columns)) ** 2)[None, None, :]
    weight = screened(squared) * (1.0 / (columns * rows * depth))
    result = jnp.zeros_like(orbitals)
    for partners in (orbitals, neighbour):
        density = (orbitals[:, None] * partners[None, :]).reshape((-1, planes, rows, columns))
        value = jnp.einsum("pzyx,xk->pzyk", density, cas_x, precision=highest)
        value = jnp.einsum("pzyx,yk->pzkx", value, cas_y, precision=highest)
        value = exchange_sum(value, split_axis, 1)
        value = jnp.einsum("pzyx,zk->pkyx", value, cas_z, precision=highest) * weight
        value = jnp.einsum("pzyx,zk->pkyx", value, cas_z, precision=highest)
        value = exchange_sum(value, 1, split_axis)
        value = jnp.einsum("pzyx,yk->pzkx", value, cas_y, precision=highest)
        value = jnp.einsum("pzyx,xk->pzyk", value, cas_x, precision=highest)
        field = value.reshape((count, count, planes, rows, columns))
        result = result - jnp.sum(field * partners[None], axis=1)
    return result


def body(orbitals, layered):
    return layered_body(orbitals) if layered else plain_body(orbitals)


def solution(mesh):
    slabs, blocks = mesh.shape["slab"], mesh.shape["band"]

    def run(orbitals):
        count, planes = orbitals.shape[0] // blocks, orbitals.shape[1] // slabs
        rows, columns = orbitals.shape[2:]
        inner = max(slabs // blocks, 1)
        share = rows // (inner * blocks)
        fits = slabs % blocks == 0 and planes % blocks == 0 and planes % 8 == 0
        fits = fits and rows % (inner * blocks) == 0 and share % 8 == 0 and columns % 128 == 0
        if fits:
            grid = mesh.devices.reshape(blocks, inner, blocks)
            finer = Mesh(grid, ("layer", "inner", "band"))
            spec = P("band", ("layer", "inner"), None, None)
            inside = layered_body
        else:
            finer, spec, inside = mesh, P("band", "slab", None, None), plain_body
        return jax.shard_map(
            inside, mesh=finer, in_specs=(spec,), out_specs=spec, check_vma=False
        )(orbitals)

    return run
```

```python
import functools
import math

import jax
import jax.numpy as jnp
from jax import lax
from jax.experimental import pallas as pl
from jax.experimental.pallas import tpu as pltpu
from jax.sharding import Mesh, PartitionSpec as P

screen_width = 0.5
highest = lax.Precision.HIGHEST


def frequency(counter, length):
    return jnp.where(counter < length // 2, counter, counter - length).astype(jnp.float32)


def screened(squared):
    safe_sq = jnp.where(squared > 0, squared, 1.0)
    value = 4.0 * math.pi / safe_sq * (1.0 - jnp.exp(-safe_sq / (4.0 * screen_width**2)))
    return jnp.where(squared > 0, value, math.pi / screen_width**2)


def cas_table(rows, columns, length):
    product = rows[:, None] * columns[None, :] % length
    angles = 2.0 * math.pi / length * product.astype(jnp.float32)
    return jnp.cos(angles) + jnp.sin(angles)


def halves(value):
    high = value.astype(jnp.bfloat16)
    return high, (value - high.astype(jnp.float32)).astype(jnp.bfloat16)


def table_halves(table):
    high = lax.reduce_precision(table, exponent_bits=8, mantissa_bits=7)
    return high.astype(jnp.bfloat16), (table - high).astype(jnp.bfloat16)


def right_table(table):
    high, low = table_halves(table)
    top = jnp.concatenate([high, low], axis=1)
    return jnp.concatenate([top, jnp.concatenate([high, jnp.zeros_like(low)], axis=1)], axis=0)


def left_table(table):
    high, low = table_halves(table)
    top = jnp.concatenate([high, high], axis=1)
    return jnp.concatenate([top, jnp.concatenate([low, jnp.zeros_like(low)], axis=1)], axis=0)


def times_right(value, table):
    width = value.shape[1]
    high, low = halves(value)
    both = jnp.dot(
        jnp.concatenate([high, low], axis=1), table, preferred_element_type=jnp.float32
    )
    return both[:, :width] + both[:, width:]


def times_left(table, value):
    high, low = halves(value)
    both = jnp.dot(
        table, jnp.concatenate([high, low], axis=0), preferred_element_type=jnp.float32
    )
    rows = both.shape[0] // 2
    return both[:rows] + both[rows:]


def forward_kernel(group, left_ref, right_ref, *refs):
    out_ref = refs[-1]
    planes, rows, columns = refs[0].shape
    share = rows // group
    for which in range(len(refs) // 2):
        first_ref, second_ref = refs[2 * which], refs[2 * which + 1]
        for plane in range(0, planes, 2):
            density = first_ref[plane : plane + 2] * second_ref[plane : plane + 2]
            part = times_right(density.reshape(2 * rows, columns), right_ref[...])
            part = times_left(left_ref[...], jnp.concatenate([part[:rows], part[rows:]], axis=1))
            for offset in range(2):
                piece = part[:, offset * columns : (offset + 1) * columns]
                for chunk in range(group):
                    out_ref[chunk, which, pl.ds(plane + offset, share, stride=planes), :] = piece[
                        chunk * share : (chunk + 1) * share
                    ]


def depth_kernel(planes, forth_ref, back_ref, weight_ref, in_ref, *out_refs):
    group = in_ref.shape[0]
    share = in_ref.shape[2] // planes
    columns = in_ref.shape[3]
    for row in range(0, share, 2):
        value = jnp.concatenate(
            [
                jnp.concatenate(
                    [
                        in_ref[chunk, 0, (row + offset) * planes : (row + offset + 1) * planes, :]
                        for chunk in range(group)
                    ],
                    axis=0,
                )
                for offset in range(2)
            ],
            axis=1,
        )
        value = times_left(forth_ref[...], value) * weight_ref[row // 2]
        value = times_left(back_ref[...], value)
        for offset in range(2):
            for chunk in range(group):
                out_refs[chunk][0, (row + offset) * planes : (row + offset + 1) * planes, :] = value[
                    chunk * planes : (chunk + 1) * planes,
                    offset * columns : (offset + 1) * columns,
                ]


def potential_planes(plane, planes, which, left_ref, right_ref, in_refs):
    columns = in_refs[0].shape[2]
    share = in_refs[0].shape[1] // planes
    rows = len(in_refs) * share
    value = jnp.concatenate(
        [
            jnp.concatenate(
                [ref[which, pl.ds(plane + offset, share, stride=planes), :] for ref in in_refs],
                axis=0,
            )
            for offset in range(2)
        ],
        axis=1,
    )
    value = times_left(left_ref[...], value)
    value = jnp.concatenate([value[:, :columns], value[:, columns:]], axis=0)
    return times_right(value, right_ref[...]).reshape(2, rows, columns)


def inverse_kernel(uses, names, planes, group, left_ref, right_ref, *refs):
    factors, held, targets, pieces = names
    in_refs, refs = refs[:group], refs[group:]
    factor_refs, refs = dict(zip(factors, refs)), refs[len(factors) :]
    held_refs, refs = dict(zip(held, refs)), refs[len(held) :]
    out_refs = {
        target: refs[place * pieces : (place + 1) * pieces] for place, target in enumerate(targets)
    }
    piece = planes // pieces
    for plane in range(0, planes, 2):
        total = {target: held_refs[target][plane : plane + 2] for target in held}
        for which, pairs in enumerate(uses):
            field = potential_planes(plane, planes, which, left_ref, right_ref, in_refs)
            for target, factor in pairs:
                term = field * factor_refs[factor][plane : plane + 2]
                total[target] = total[target] - term if target in total else -term
        for target in targets:
            spot = plane % piece
            out_refs[target][plane // piece][spot : spot + 2] = total[target]


def whole(shape):
    return pl.BlockSpec(shape, lambda *grid: (0,) * len(shape))


def cost(steps):
    return pl.CostEstimate(flops=steps * 700_000_000, bytes_accessed=steps * 3_000_000, transcendentals=0)


def forward(pairs, group, left, right):
    planes, rows, columns = pairs[0][0].shape
    lines = rows // group * planes
    return pl.pallas_call(
        functools.partial(forward_kernel, group),
        out_shape=jax.ShapeDtypeStruct((group, len(pairs), lines, columns), jnp.float32),
        cost_estimate=cost(len(pairs)),
        name="forward",
    )(left, right, *[orbital for pair in pairs for orbital in pair])


def through_depth(value, planes, forth, back, weight):
    group, count, lines, columns = value.shape
    return pl.pallas_call(
        functools.partial(depth_kernel, planes),
        grid=(count,),
        in_specs=[
            whole(forth.shape),
            whole(back.shape),
            whole(weight.shape),
            pl.BlockSpec((group, 1, lines, columns), lambda step: (0, step, 0, 0)),
        ],
        out_specs=[pl.BlockSpec((1, lines, columns), lambda step: (step, 0, 0))] * group,
        out_shape=[jax.ShapeDtypeStruct((count, lines, columns), jnp.float32)] * group,
        cost_estimate=cost(count),
        name="through_depth",
    )(forth, back, weight, value)


def inverse(values, uses, orbitals, held, pieces, left, right):
    factors = sorted({factor for pairs in uses for _, factor in pairs})
    targets = sorted({target for pairs in uses for target, _ in pairs})
    given = [target for target in targets if target in held]
    planes, rows, columns = orbitals[factors[0]].shape
    piece = jax.ShapeDtypeStruct((planes // pieces, rows, columns), jnp.float32)
    names = (factors, given, targets, pieces)
    results = pl.pallas_call(
        functools.partial(inverse_kernel, uses, names, planes, len(values)),
        out_shape=[piece] * (pieces * len(targets)),
        cost_estimate=cost(len(uses)),
        name="inverse",
    )(
        left,
        right,
        *values,
        *[orbitals[factor] for factor in factors],
        *[held[target] for target in given],
    )
    return {
        target: results[place * pieces : (place + 1) * pieces]
        for place, target in enumerate(targets)
    }


def layered_body(orbitals):
    blocks = lax.axis_size("band")
    inner = lax.axis_size("inner")
    count, planes, rows, columns = orbitals.shape
    piece = planes // blocks
    group = inner * blocks
    depth = planes * inner * blocks
    share = rows // group
    layer = lax.axis_index("layer")
    band = lax.axis_index("band")
    me = lax.axis_index(("inner", "band"))

    split = orbitals.reshape(count, blocks, piece, rows, columns)
    own = []
    for index in range(count):
        moved = lax.all_to_all(split[index], "band", split_axis=0, concat_axis=0, tiled=True)
        gathered = jnp.zeros((blocks, piece, rows, columns), jnp.float32)
        for step in range(blocks):
            part = lax.dynamic_index_in_dim(moved, layer ^ step, 0, keepdims=True)
            if step:
                pairs = [(source, source ^ step) for source in range(blocks)]
                part = lax.ppermute(part, "layer", pairs)
            gathered = lax.dynamic_update_index_in_dim(gathered, part, layer ^ step ^ band, 0)
        own.append(gathered.reshape(planes, rows, columns))
    pairs = [(source, (source + 1) % blocks) for source in range(blocks)]
    other = [lax.ppermute(orbital, "layer", pairs) for orbital in own]
    known = own + other

    counter = jnp.arange(columns, dtype=jnp.int32)
    across = right_table(cas_table(counter, counter, columns))
    counter = jnp.arange(rows, dtype=jnp.int32)
    along = left_table(cas_table(counter, counter, rows))
    held_rows = (counter // share ^ me) * share + counter % share
    along_back = left_table(cas_table(counter, held_rows, rows))
    counter = jnp.arange(depth, dtype=jnp.int32)

    def place(source):
        local = counter % planes
        spot = (local // piece ^ source % blocks) * (inner * planes) + source // blocks * planes
        return spot + source % blocks * piece + local % piece

    forth = left_table(cas_table(counter, place(counter // planes), depth))
    back = left_table(cas_table(place(counter // planes ^ me), counter, depth))

    freq_z = 2.0 * math.pi / depth * frequency(counter, depth)
    mine = me * share + jnp.arange(share, dtype=jnp.int32)
    freq_y = 2.0 * math.pi / rows * frequency(mine, rows)
    freq_x = 2.0 * math.pi / columns * frequency(jnp.arange(columns, dtype=jnp.int32), columns)
    squared = (freq_y**2).reshape(share // 2, 1, 2, 1) + (freq_z**2)[None, :, None, None]
    squared = squared + (freq_x**2)[None, None, None, :]
    weight = screened(squared) * (1.0 / (columns * rows * depth))
    weight = weight.reshape(share // 2, depth, 2 * columns)

    axes = ("inner", "band")

    def forth_exchange(value):
        return lax.all_to_all(value, axes, split_axis=0, concat_axis=0, tiled=True)

    def back_exchange(values):
        return [
            lax.ppermute(value, axes, [(source, source ^ step) for source in range(group)])
            if step
            else value
            for step, value in enumerate(values)
        ]

    batches = [[(0, 0)]] + [[(i, j) for i in range(j + 1)] for j in range(1, count)]
    batches += [[(i, count + j) for j in range(count)] for i in range(count)]
    last = {i: len(batches) - count + i for i in range(count)}
    held = {}
    for order, batch in enumerate(batches):
        value = forward([(known[i], known[j]) for i, j in batch], group, along, across)
        value = forth_exchange(value)
        values = through_depth(value, planes, forth, back, weight)
        values = back_exchange(values)
        uses = [[(i, j)] + ([(j, i)] if i != j < count else []) for i, j in batch]
        done = order >= len(batches) - count
        results = inverse(values, uses, known, held, blocks if done else 1, along_back, across)
        held.update({target: parts if done else parts[0] for target, parts in results.items()})

    everywhere = ("layer", "inner", "band")

    def route(step):
        spot = lambda at, within, along: (at * inner + within) * blocks + along
        return [
            (spot(q, i, b), spot(b ^ step, i, q))
            for q in range(blocks)
            for i in range(inner)
            for b in range(blocks)
        ]

    out = jnp.zeros((count, blocks, piece, rows, columns), jnp.float32)
    for index in range(count):
        for step in range(blocks):
            part = lax.ppermute(held[index][step], everywhere, route(step))
            out = lax.dynamic_update_slice(out, part[None, None], (index, layer ^ step, 0, 0, 0))
    return out.reshape(count, planes, rows, columns)


def exchange_sum(value, split_axis, concat_axis):
    return lax.all_to_all(value, "slab", split_axis=split_axis, concat_axis=concat_axis, tiled=True)


def plain_body(orbitals):
    count, planes, rows, columns = orbitals.shape
    depth = planes * lax.axis_size("slab")
    blocks = lax.axis_size("band")
    pairs = [(source, (source + 1) % blocks) for source in range(blocks)]
    neighbour = lax.ppermute(orbitals, "band", pairs)
    x_count = jnp.arange(columns, dtype=jnp.int32)
    y_count = jnp.arange(rows, dtype=jnp.int32)
    z_count = jnp.arange(depth, dtype=jnp.int32)
    cas_x = cas_table(x_count, x_count, columns)
    cas_y = cas_table(y_count, y_count, rows)
    cas_z = cas_table(z_count, z_count, depth)
    slabs = lax.axis_size("slab")
    split_axis, extent = (2, rows) if rows % slabs == 0 else (3, columns)
    share = extent // slabs
    mine = lax.axis_index("slab") * share + jnp.arange(share, dtype=jnp.int32)
    y_rows, x_rows = (mine, x_count) if split_axis == 2 else (y_count, mine)
    squared = ((2.0 * math.pi / depth * frequency(z_count, depth)) ** 2)[:, None, None]
    squared = squared + ((2.0 * math.pi / rows * frequency(y_rows, rows)) ** 2)[None, :, None]
    squared = squared + ((2.0 * math.pi / columns * frequency(x_rows, columns)) ** 2)[None, None, :]
    weight = screened(squared) * (1.0 / (columns * rows * depth))
    result = jnp.zeros_like(orbitals)
    for partners in (orbitals, neighbour):
        density = (orbitals[:, None] * partners[None, :]).reshape((-1, planes, rows, columns))
        value = jnp.einsum("pzyx,xk->pzyk", density, cas_x, precision=highest)
        value = jnp.einsum("pzyx,yk->pzkx", value, cas_y, precision=highest)
        value = exchange_sum(value, split_axis, 1)
        value = jnp.einsum("pzyx,zk->pkyx", value, cas_z, precision=highest) * weight
        value = jnp.einsum("pzyx,zk->pkyx", value, cas_z, precision=highest)
        value = exchange_sum(value, 1, split_axis)
        value = jnp.einsum("pzyx,yk->pzkx", value, cas_y, precision=highest)
        value = jnp.einsum("pzyx,xk->pzyk", value, cas_x, precision=highest)
        field = value.reshape((count, count, planes, rows, columns))
        result = result - jnp.sum(field * partners[None], axis=1)
    return result


def body(orbitals, layered):
    return layered_body(orbitals) if layered else plain_body(orbitals)


def solution(mesh):
    slabs, blocks = mesh.shape["slab"], mesh.shape["band"]

    def run(orbitals):
        count, planes = orbitals.shape[0] // blocks, orbitals.shape[1] // slabs
        rows, columns = orbitals.shape[2:]
        inner = max(slabs // blocks, 1)
        share = rows // (inner * blocks)
        fits = slabs % blocks == 0 and planes % (2 * blocks) == 0 and planes % 8 == 0
        fits = fits and slabs & (slabs - 1) == 0 and blocks & (blocks - 1) == 0
        fits = fits and rows % (inner * blocks) == 0 and share % 8 == 0 and columns % 128 == 0
        if fits:
            grid = mesh.devices.reshape(blocks, inner, blocks)
            finer = Mesh(grid, ("layer", "inner", "band"))
            spec = P("band", ("layer", "inner"), None, None)
            inside = layered_body
        else:
            finer, spec, inside = mesh, P("band", "slab", None, None), plain_body
        return jax.shard_map(
            inside, mesh=finer, in_specs=(spec,), out_specs=spec, check_vma=False
        )(orbitals)

    return run
```

```python
import functools
import math

import jax
import jax.numpy as jnp
from jax import lax
from jax.experimental import pallas as pl
from jax.experimental.pallas import tpu as pltpu
from jax.sharding import Mesh, PartitionSpec as P

screen_width = 0.5
highest = lax.Precision.HIGHEST


def frequency(counter, length):
    return jnp.where(counter < length // 2, counter, counter - length).astype(jnp.float32)


def screened(squared):
    safe_sq = jnp.where(squared > 0, squared, 1.0)
    value = 4.0 * math.pi / safe_sq * (1.0 - jnp.exp(-safe_sq / (4.0 * screen_width**2)))
    return jnp.where(squared > 0, value, math.pi / screen_width**2)


def cas_table(rows, columns, length):
    product = rows[:, None] * columns[None, :] % length
    angles = 2.0 * math.pi / length * product.astype(jnp.float32)
    return jnp.cos(angles) + jnp.sin(angles)


def halves(value):
    high = value.astype(jnp.bfloat16)
    return high, (value - high.astype(jnp.float32)).astype(jnp.bfloat16)


def table_halves(table):
    high = lax.reduce_precision(table, exponent_bits=8, mantissa_bits=7)
    return high.astype(jnp.bfloat16), (table - high).astype(jnp.bfloat16)


def right_table(table):
    high, low = table_halves(table)
    top = jnp.concatenate([high, low], axis=1)
    return jnp.concatenate([top, jnp.concatenate([high, jnp.zeros_like(low)], axis=1)], axis=0)


def left_table(table):
    high, low = table_halves(table)
    top = jnp.concatenate([high, high], axis=1)
    return jnp.concatenate([top, jnp.concatenate([low, jnp.zeros_like(low)], axis=1)], axis=0)


def times_right(value, table):
    width = value.shape[1]
    high, low = halves(value)
    both = jnp.dot(
        jnp.concatenate([high, low], axis=1), table, preferred_element_type=jnp.float32
    )
    return both[:, :width] + both[:, width:]


def times_left(table, value):
    high, low = halves(value)
    both = jnp.dot(
        table, jnp.concatenate([high, low], axis=0), preferred_element_type=jnp.float32
    )
    rows = both.shape[0] // 2
    return both[:rows] + both[rows:]


def forward_kernel(group, pieces, pairs, left_ref, right_ref, *refs):
    refs, out_refs = refs[:-group], refs[-group:]
    piece, rows, columns = refs[0].shape
    share = rows // group
    planes = piece * pieces
    for which, (first, second) in enumerate(pairs):
        for plane in range(0, planes, 2):
            slot, spot = plane // piece, slice(plane % piece, plane % piece + 2)
            density = refs[first * pieces + slot][spot] * refs[second * pieces + slot][spot]
            part = times_right(density.reshape(2 * rows, columns), right_ref[...])
            part = times_left(left_ref[...], jnp.concatenate([part[:rows], part[rows:]], axis=1))
            for offset in range(2):
                lines = part[:, offset * columns : (offset + 1) * columns]
                for chunk in range(group):
                    out_refs[chunk][which, pl.ds(plane + offset, share, stride=planes), :] = lines[
                        chunk * share : (chunk + 1) * share
                    ]


def depth_kernel(planes, forth_ref, back_ref, weight_ref, *refs):
    group = len(refs) // 2
    in_refs, out_refs = refs[:group], refs[group:]
    share = in_refs[0].shape[1] // planes
    columns = in_refs[0].shape[2]
    for row in range(0, share, 2):
        lines = [slice((row + offset) * planes, (row + offset + 1) * planes) for offset in range(2)]
        value = jnp.concatenate(
            [jnp.concatenate([ref[0, span, :] for ref in in_refs], axis=0) for span in lines],
            axis=1,
        )
        value = times_left(forth_ref[...], value) * weight_ref[row // 2]
        value = times_left(back_ref[...], value)
        for offset, span in enumerate(lines):
            for chunk in range(group):
                out_refs[chunk][0, span, :] = value[
                    chunk * planes : (chunk + 1) * planes,
                    offset * columns : (offset + 1) * columns,
                ]


def potential_planes(plane, planes, which, left_ref, right_ref, in_refs):
    columns = in_refs[0].shape[2]
    share = in_refs[0].shape[1] // planes
    rows = len(in_refs) * share
    value = jnp.concatenate(
        [
            jnp.concatenate(
                [ref[which, pl.ds(plane + offset, share, stride=planes), :] for ref in in_refs],
                axis=0,
            )
            for offset in range(2)
        ],
        axis=1,
    )
    value = times_left(left_ref[...], value)
    value = jnp.concatenate([value[:, :columns], value[:, columns:]], axis=0)
    return times_right(value, right_ref[...]).reshape(2, rows, columns)


def inverse_kernel(uses, names, pieces, group, left_ref, right_ref, *refs):
    factors, held, targets = names
    in_refs, refs = refs[:group], refs[group:]
    factor_refs = {
        factor: refs[place * pieces : (place + 1) * pieces] for place, factor in enumerate(factors)
    }
    refs = refs[len(factors) * pieces :]
    held_refs, out_refs = dict(zip(held, refs)), dict(zip(targets, refs[len(held) :]))
    planes = refs[-1].shape[0]
    piece = planes // pieces
    for plane in range(0, planes, 2):
        both = slice(plane, plane + 2)
        slot, spot = plane // piece, slice(plane % piece, plane % piece + 2)
        total = {target: held_refs[target][both] for target in held}
        for which, pairs in enumerate(uses):
            field = potential_planes(plane, planes, which, left_ref, right_ref, in_refs)
            for target, factor in pairs:
                term = field * factor_refs[factor][slot][spot]
                total[target] = total[target] - term if target in total else -term
        for target in targets:
            out_refs[target][both] = total[target]


def whole(shape):
    return pl.BlockSpec(shape, lambda *grid: (0,) * len(shape))


def cost(steps):
    return pl.CostEstimate(flops=steps * 700_000_000, bytes_accessed=steps * 3_000_000, transcendentals=0)


def forward(pairs, known, group, left, right):
    used = sorted({index for pair in pairs for index in pair})
    pieces = len(known[used[0]])
    piece, rows, columns = known[used[0]][0].shape
    chunk = jax.ShapeDtypeStruct((len(pairs), rows // group * piece * pieces, columns), jnp.float32)
    places = [(used.index(first), used.index(second)) for first, second in pairs]
    return pl.pallas_call(
        functools.partial(forward_kernel, group, pieces, places),
        out_shape=[chunk] * group,
        cost_estimate=cost(len(pairs)),
        name="forward",
    )(left, right, *[part for index in used for part in known[index]])


def through_depth(values, planes, forth, back, weight):
    count, lines, columns = values[0].shape
    blocks = [pl.BlockSpec((1, lines, columns), lambda step: (step, 0, 0))] * len(values)
    return pl.pallas_call(
        functools.partial(depth_kernel, planes),
        grid=(count,),
        in_specs=[whole(forth.shape), whole(back.shape), whole(weight.shape)] + blocks,
        out_specs=blocks,
        out_shape=[jax.ShapeDtypeStruct((count, lines, columns), jnp.float32)] * len(values),
        cost_estimate=cost(count),
        name="through_depth",
    )(forth, back, weight, *values)


def inverse(values, uses, known, held, left, right):
    factors = sorted({factor for pairs in uses for _, factor in pairs})
    targets = sorted({target for pairs in uses for target, _ in pairs})
    given = [target for target in targets if target in held]
    pieces = len(known[factors[0]])
    piece, rows, columns = known[factors[0]][0].shape
    result = jax.ShapeDtypeStruct((piece * pieces, rows, columns), jnp.float32)
    results = pl.pallas_call(
        functools.partial(inverse_kernel, uses, (factors, given, targets), pieces, len(values)),
        out_shape=[result] * len(targets),
        cost_estimate=cost(len(uses)),
        name="inverse",
    )(
        left,
        right,
        *values,
        *[part for factor in factors for part in known[factor]],
        *[held[target] for target in given],
    )
    return dict(zip(targets, results))


def schedule(count):
    order = [(0, 0), (1, 0), (0, 1), (2, 0), (1, 1)]
    for batch in range(2, count):
        order += [(0, batch)] + ([(2, 1)] if batch == 2 else [(1, batch - 1)])
    order += [(1, count - 1)]
    return order + [(2, batch) for batch in range(2, count)]


def after(value, *earlier):
    return lax.optimization_barrier((value,) + earlier)[0]


def layered_body(orbitals):
    blocks = lax.axis_size("band")
    inner = lax.axis_size("inner")
    count, planes, rows, columns = orbitals.shape
    piece = planes // blocks
    group = inner * blocks
    depth = planes * inner * blocks
    share = rows // group
    layer = lax.axis_index("layer")
    band = lax.axis_index("band")
    me = lax.axis_index(("inner", "band"))

    counter = jnp.arange(columns, dtype=jnp.int32)
    across = right_table(cas_table(counter, counter, columns))
    counter = jnp.arange(rows, dtype=jnp.int32)
    held_rows = (counter // share ^ me) * share + counter % share
    along_table = cas_table(held_rows, counter, rows)
    along = left_table(along_table)
    along_back = left_table(along_table.T)
    counter = jnp.arange(depth, dtype=jnp.int32)
    source, local = counter // planes ^ me, counter % planes
    place = (local // piece ^ layer) * (inner * planes) + source // blocks * planes
    place = place + source % blocks * piece + local % piece
    depth_table = cas_table(counter, place, depth)
    forth = left_table(depth_table)
    back = left_table(depth_table.T)

    freq_z = 2.0 * math.pi / depth * frequency(counter, depth)
    mine = me * share + jnp.arange(share, dtype=jnp.int32)
    freq_y = 2.0 * math.pi / rows * frequency(mine, rows)
    freq_x = 2.0 * math.pi / columns * frequency(jnp.arange(columns, dtype=jnp.int32), columns)
    squared = (freq_y**2).reshape(share // 2, 1, 2, 1) + (freq_z**2)[None, :, None, None]
    squared = squared + (freq_x**2)[None, None, None, :]
    weight = screened(squared) * (1.0 / (columns * rows * depth))
    weight = weight.reshape(share // 2, depth, 2 * columns)

    grid_shape = (blocks, piece, rows, columns)
    out = jnp.zeros((count,) + grid_shape, jnp.float32)
    moved = []
    for index in range(count):
        source = after(orbitals, across) if index else orbitals
        source = source[index].reshape(grid_shape)
        moved.append(lax.all_to_all(source, "band", split_axis=0, concat_axis=0, tiled=True))
    tables = (out, across, along, along_back, forth, back, weight)
    moved[1], out, across, along, along_back, forth, back, weight = lax.optimization_barrier(
        (moved[1],) + tables
    )

    def gather(index, shift, *earlier):
        parts = []
        for step in range(blocks):
            block = (layer ^ step) + (blocks - shift)
            part = lax.dynamic_index_in_dim(moved[index], block % blocks, 0, keepdims=False)
            if earlier:
                part = after(part, *earlier)
            if step:
                part = lax.ppermute(part, "layer", [(at, at ^ step) for at in range(blocks)])
            parts.append(part)
        return parts

    known = {}
    for index in range(count):
        known[index] = gather(index, 0, *(known[index - 1][1:] if index else ()))

    def exchange(values):
        axes = ("inner", "band")
        return [
            lax.ppermute(value, axes, [(at, at ^ step) for at in range(group)]) if step else value
            for step, value in enumerate(values)
        ]

    batches = [[(0, 0)]] + [[(i, j) for i in range(j + 1)] for j in range(1, count)]
    batches += [[(i, count + j) for j in range(count)] for i in range(count)]
    held, state = {}, {}
    previous = []

    def begin(order):
        right = after(across, *previous)
        values = forward(batches[order], known, group, along, right)
        previous[:] = values[:1]
        state[order] = exchange(values)

    def middle(order):
        weights = after(weight, *previous)
        values = through_depth(state[order], planes, forth, back, weights)
        previous[:] = values[:1]
        state[order] = exchange(values)

    def finish(order):
        right = after(across, *previous)
        uses = [[(i, j)] + ([(j, i)] if i != j < count else []) for i, j in batches[order]]
        held.update(inverse(state[order], uses, known, held, along_back, right))
        previous[:] = [held[uses[0][0][0]]]

    for act, order in schedule(len(batches)):
        if (act, order) == (0, 1):
            for index in range(count):
                known[count + index] = gather(index, 1, *known[count - 1][1:], *previous)
        (begin, middle, finish)[act](order)

    everywhere = ("layer", "inner", "band")

    def route(step):
        spot = lambda at, within, along: (at * inner + within) * blocks + along
        return [
            (spot(q, i, b), spot(b ^ step, i, q))
            for q in range(blocks)
            for i in range(inner)
            for b in range(blocks)
        ]

    for index in range(count):
        result = held[index].reshape(grid_shape)
        for step in range(blocks):
            part = lax.dynamic_index_in_dim(result, layer ^ band ^ step, 0, keepdims=False)
            part = lax.ppermute(part, everywhere, route(step))
            out = lax.dynamic_update_slice(out, part[None, None], (index, layer ^ step, 0, 0, 0))
    return out.reshape(count, planes, rows, columns)


def exchange_sum(value, split_axis, concat_axis):
    return lax.all_to_all(value, "slab", split_axis=split_axis, concat_axis=concat_axis, tiled=True)


def plain_body(orbitals):
    count, planes, rows, columns = orbitals.shape
    depth = planes * lax.axis_size("slab")
    blocks = lax.axis_size("band")
    pairs = [(source, (source + 1) % blocks) for source in range(blocks)]
    neighbour = lax.ppermute(orbitals, "band", pairs)
    x_count = jnp.arange(columns, dtype=jnp.int32)
    y_count = jnp.arange(rows, dtype=jnp.int32)
    z_count = jnp.arange(depth, dtype=jnp.int32)
    cas_x = cas_table(x_count, x_count, columns)
    cas_y = cas_table(y_count, y_count, rows)
    cas_z = cas_table(z_count, z_count, depth)
    slabs = lax.axis_size("slab")
    split_axis, extent = (2, rows) if rows % slabs == 0 else (3, columns)
    share = extent // slabs
    mine = lax.axis_index("slab") * share + jnp.arange(share, dtype=jnp.int32)
    y_rows, x_rows = (mine, x_count) if split_axis == 2 else (y_count, mine)
    squared = ((2.0 * math.pi / depth * frequency(z_count, depth)) ** 2)[:, None, None]
    squared = squared + ((2.0 * math.pi / rows * frequency(y_rows, rows)) ** 2)[None, :, None]
    squared = squared + ((2.0 * math.pi / columns * frequency(x_rows, columns)) ** 2)[None, None, :]
    weight = screened(squared) * (1.0 / (columns * rows * depth))
    result = jnp.zeros_like(orbitals)
    for partners in (orbitals, neighbour):
        density = (orbitals[:, None] * partners[None, :]).reshape((-1, planes, rows, columns))
        value = jnp.einsum("pzyx,xk->pzyk", density, cas_x, precision=highest)
        value = jnp.einsum("pzyx,yk->pzkx", value, cas_y, precision=highest)
        value = exchange_sum(value, split_axis, 1)
        value = jnp.einsum("pzyx,zk->pkyx", value, cas_z, precision=highest) * weight
        value = jnp.einsum("pzyx,zk->pkyx", value, cas_z, precision=highest)
        value = exchange_sum(value, 1, split_axis)
        value = jnp.einsum("pzyx,yk->pzkx", value, cas_y, precision=highest)
        value = jnp.einsum("pzyx,xk->pzyk", value, cas_x, precision=highest)
        field = value.reshape((count, count, planes, rows, columns))
        result = result - jnp.sum(field * partners[None], axis=1)
    return result


def body(orbitals, layered):
    return layered_body(orbitals) if layered else plain_body(orbitals)


def solution(mesh):
    slabs, blocks = mesh.shape["slab"], mesh.shape["band"]

    def run(orbitals):
        count, planes = orbitals.shape[0] // blocks, orbitals.shape[1] // slabs
        rows, columns = orbitals.shape[2:]
        inner = max(slabs // blocks, 1)
        share = rows // (inner * blocks)
        fits = slabs % blocks == 0 and planes % (2 * blocks) == 0 and planes % 8 == 0
        fits = fits and slabs & (slabs - 1) == 0 and blocks & (blocks - 1) == 0
        fits = fits and rows % (inner * blocks) == 0 and share % 8 == 0 and columns % 128 == 0
        if fits:
            grid = mesh.devices.reshape(blocks, inner, blocks)
            finer = Mesh(grid, ("layer", "inner", "band"))
            spec = P("band", ("layer", "inner"), None, None)
            inside = layered_body
        else:
            finer, spec, inside = mesh, P("band", "slab", None, None), plain_body
        return jax.shard_map(
            inside, mesh=finer, in_specs=(spec,), out_specs=spec, check_vma=False
        )(orbitals)

    return run
```

```python
import functools
import math

import jax
import jax.numpy as jnp
from jax import lax
from jax.experimental import pallas as pl
from jax.experimental.pallas import tpu as pltpu
from jax.sharding import Mesh, PartitionSpec as P


screen_width = 0.5
highest = lax.Precision.HIGHEST


def frequency(counter, length):
    return jnp.where(counter < length // 2, counter, counter - length).astype(jnp.float32)


def screened(squared):
    safe_sq = jnp.where(squared > 0, squared, 1.0)
    value = 4.0 * math.pi / safe_sq * (1.0 - jnp.exp(-safe_sq / (4.0 * screen_width**2)))
    return jnp.where(squared > 0, value, math.pi / screen_width**2)


def cas_table(rows, columns, length):
    product = rows[:, None] * columns[None, :] % length
    angles = 2.0 * math.pi / length * product.astype(jnp.float32)
    return jnp.cos(angles) + jnp.sin(angles)


def halves(value):
    high = value.astype(jnp.bfloat16)
    return high, (value - high.astype(jnp.float32)).astype(jnp.bfloat16)


def table_halves(table):
    high = lax.reduce_precision(table, exponent_bits=8, mantissa_bits=7)
    return high.astype(jnp.bfloat16), (table - high).astype(jnp.bfloat16)


def right_table(table):
    high, low = table_halves(table)
    top = jnp.concatenate([high, low], axis=1)
    return jnp.concatenate([top, jnp.concatenate([high, jnp.zeros_like(low)], axis=1)], axis=0)


def left_table(table):
    high, low = table_halves(table)
    top = jnp.concatenate([high, high], axis=1)
    return jnp.concatenate([top, jnp.concatenate([low, jnp.zeros_like(low)], axis=1)], axis=0)


def times_right(value, table):
    width = value.shape[1]
    high, low = halves(value)
    both = jnp.dot(
        jnp.concatenate([high, low], axis=1), table, preferred_element_type=jnp.float32
    )
    return both[:, :width] + both[:, width:]


def times_left(table, value):
    high, low = halves(value)
    both = jnp.dot(
        table, jnp.concatenate([high, low], axis=0), preferred_element_type=jnp.float32
    )
    rows = both.shape[0] // 2
    return both[:rows] + both[rows:]


def spot_of(plane, planes, pieces):
    half, reach = planes // 2, planes // pieces // 2
    return plane % half // reach, plane // half * reach + plane % reach


def pair_at(refs, plane, planes, pieces):
    piece, place = spot_of(plane, planes, pieces)
    return refs[piece][place : place + 2]


def forward_kernel(group, pieces, pairs, left_ref, right_ref, *refs):
    refs, out_refs = refs[:-group], refs[-group:]
    piece, rows, columns = refs[0].shape
    share = rows // group
    planes = piece * pieces
    orbitals = [refs[at : at + pieces] for at in range(0, len(refs), pieces)]
    for which, (first, second) in enumerate(pairs):
        for plane in range(0, planes, 2):
            density = pair_at(orbitals[first], plane, planes, pieces)
            density = density * pair_at(orbitals[second], plane, planes, pieces)
            part = times_right(density.reshape(2 * rows, columns), right_ref[...])
            part = times_left(left_ref[...], jnp.concatenate([part[:rows], part[rows:]], axis=1))
            for offset in range(2):
                lines = part[:, offset * columns : (offset + 1) * columns]
                for chunk in range(group):
                    out_refs[chunk][which, pl.ds(plane + offset, share, stride=planes), :] = lines[
                        chunk * share : (chunk + 1) * share
                    ]


def depth_kernel(planes, group, forth_ref, back_ref, weight_ref, *refs):
    in_refs, out_refs = refs[:group], refs[group:]
    parts = len(out_refs) // group
    reach = planes // parts
    share = in_refs[0].shape[1] // planes
    columns = in_refs[0].shape[2]
    for row in range(0, share, 2):
        value = jnp.concatenate(
            [
                jnp.concatenate(
                    [ref[0, at * planes : (at + 1) * planes, :] for ref in in_refs], axis=0
                )
                for at in (row, row + 1)
            ],
            axis=1,
        )
        value = times_left(forth_ref[...], value) * weight_ref[row // 2]
        value = times_left(back_ref[...], value)
        for offset, at in enumerate((row, row + 1)):
            for place, ref in enumerate(out_refs):
                first = place % group * planes + place // group * reach
                ref[0, at * reach : (at + 1) * reach, :] = value[
                    first : first + reach, offset * columns : (offset + 1) * columns
                ]


def potential_planes(plane, planes, which, left_ref, right_ref, in_refs):
    columns = in_refs[0].shape[2]
    share = in_refs[0].shape[1] // planes
    rows = len(in_refs) * share
    value = jnp.concatenate(
        [
            jnp.concatenate(
                [ref[which, pl.ds(plane + offset, share, stride=planes), :] for ref in in_refs],
                axis=0,
            )
            for offset in range(2)
        ],
        axis=1,
    )
    value = times_left(left_ref[...], value)
    value = jnp.concatenate([value[:, :columns], value[:, columns:]], axis=0)
    return times_right(value, right_ref[...]).reshape(2, rows, columns)


def inverse_kernel(uses, names, pieces, group, begin, left_ref, right_ref, *refs):
    factors, held, targets = names
    in_refs, refs = refs[:group], refs[group:]
    factor_refs = {
        factor: refs[place * pieces : (place + 1) * pieces] for place, factor in enumerate(factors)
    }
    planes = refs[0].shape[0] * pieces
    refs = refs[len(factors) * pieces :]
    held_refs, out_refs = dict(zip(held, refs)), dict(zip(targets, refs[len(held) :]))
    count = refs[-1].shape[0]
    for plane in range(0, count, 2):
        total = {target: held_refs[target][begin + plane : begin + plane + 2] for target in held}
        for which, pairs in enumerate(uses):
            field = potential_planes(plane, count, which, left_ref, right_ref, in_refs)
            for target, factor in pairs:
                term = field * pair_at(factor_refs[factor], begin + plane, planes, pieces)
                total[target] = total[target] - term if target in total else -term
        for target in targets:
            out_refs[target][plane : plane + 2] = total[target]


grant = pltpu.CompilerParams(vmem_limit_bytes=16 * 1024 * 1024)


def whole(shape):
    return pl.BlockSpec(shape, lambda *grid: (0,) * len(shape))


def cost(steps):
    return pl.CostEstimate(flops=steps * 700_000_000, bytes_accessed=steps * 3_000_000, transcendentals=0)


def forward(pairs, known, group, left, right):
    used = sorted({index for pair in pairs for index in pair})
    pieces = len(known[used[0]])
    piece, rows, columns = known[used[0]][0].shape
    chunk = jax.ShapeDtypeStruct((len(pairs), rows // group * piece * pieces, columns), jnp.float32)
    places = [(used.index(first), used.index(second)) for first, second in pairs]
    return pl.pallas_call(
        functools.partial(forward_kernel, group, pieces, places),
        out_shape=[chunk] * group,
        cost_estimate=cost(len(pairs)),
        compiler_params=grant,
        name="forward",
    )(left, right, *[part for index in used for part in known[index]])


def through_depth(values, planes, parts, forth, back, weight):
    count, lines, columns = values[0].shape
    group, reach = len(values), lines // parts

    def block(size):
        return pl.BlockSpec((1, size, columns), lambda step: (step, 0, 0))

    return pl.pallas_call(
        functools.partial(depth_kernel, planes, group),
        grid=(count,),
        in_specs=[whole(forth.shape), whole(back.shape), whole(weight.shape)]
        + [block(lines)] * group,
        out_specs=[block(reach)] * (group * parts),
        out_shape=[jax.ShapeDtypeStruct((count, reach, columns), jnp.float32)] * (group * parts),
        cost_estimate=cost(count),
        compiler_params=grant,
        name="through_depth",
    )(forth, back, weight, *values)


def inverse(values, uses, known, held, begin, left, right):
    factors = sorted({factor for pairs in uses for _, factor in pairs})
    targets = sorted({target for pairs in uses for target, _ in pairs})
    given = [target for target in targets if target in held]
    pieces = len(known[factors[0]])
    _, rows, columns = known[factors[0]][0].shape
    planes = values[0].shape[1] * len(values) // rows
    result = jax.ShapeDtypeStruct((planes, rows, columns), jnp.float32)
    names = (factors, given, targets)
    results = pl.pallas_call(
        functools.partial(inverse_kernel, uses, names, pieces, len(values), begin),
        out_shape=[result] * len(targets),
        cost_estimate=cost(len(uses)),
        compiler_params=grant,
        name="inverse",
    )(
        left,
        right,
        *values,
        *[part for factor in factors for part in known[factor]],
        *[held[target] for target in given],
    )
    return dict(zip(targets, results))


def batch_list(count):
    batches = [[(i, j)] for j in range(count) for i in range(j + 1)]
    batches += [[(i, count + j)] for i in range(count - 1) for j in range(count)]
    return batches + [[(count - 1, count + j) for j in range(count)]]


def schedule(count):
    total = len(batch_list(count))
    own, last = count * (count + 1) // 2, total - 1
    order = ["f0", "d0"] + [f"f{batch}" for batch in range(1, own)] + ["i0"]
    order += [f"d{batch}" for batch in range(1, own)]
    for batch in range(own, last):
        order += [f"f{batch}"] + ([f"i{batch - own + 1}"] if batch - own + 1 < own else [])
    order += [f"i{batch}" for batch in range(last - own + 1, own)]
    order += [f"d{own}", f"f{last}"] + [f"d{batch}" for batch in range(own + 1, last)]
    order += [f"i{batch}" for batch in range(own, last - 1)]
    return order + [f"d{last}", f"i{last - 1}", f"i{last}", f"i{last}b"]


def after(value, *earlier):
    return lax.optimization_barrier((value,) + earlier)[0]


def layered_body(orbitals):
    blocks = lax.axis_size("band")
    inner = lax.axis_size("inner")
    count, planes, rows, columns = orbitals.shape
    piece = planes // blocks
    group = inner * blocks
    depth = planes * inner * blocks
    share = rows // group
    layer = lax.axis_index("layer")
    band = lax.axis_index("band")
    me = lax.axis_index(("inner", "band"))

    counter = jnp.arange(columns, dtype=jnp.int32)
    across = right_table(cas_table(counter, counter, columns))
    counter = jnp.arange(rows, dtype=jnp.int32)
    held_rows = (counter // share ^ me) * share + counter % share
    along_table = cas_table(held_rows, counter, rows)
    along = left_table(along_table)
    along_back = left_table(along_table.T)
    counter = jnp.arange(depth, dtype=jnp.int32)
    source, local = counter // planes ^ me, counter % planes
    slot, offset = spot_of(local, planes, blocks)
    place = (slot ^ layer) * (inner * planes) + source // blocks * planes
    place = place + source % blocks * piece + offset
    depth_table = cas_table(counter, place, depth)
    forth = left_table(depth_table)
    back = left_table(depth_table.T)

    freq_z = 2.0 * math.pi / depth * frequency(counter, depth)
    mine = me * share + jnp.arange(share, dtype=jnp.int32)
    freq_y = 2.0 * math.pi / rows * frequency(mine, rows)
    freq_x = 2.0 * math.pi / columns * frequency(jnp.arange(columns, dtype=jnp.int32), columns)
    squared = (freq_y**2).reshape(share // 2, 1, 2, 1) + (freq_z**2)[None, :, None, None]
    squared = squared + (freq_x**2)[None, None, None, :]
    weight = screened(squared) * (1.0 / (columns * rows * depth))
    weight = weight.reshape(share // 2, depth, 2 * columns)

    grid_shape = (blocks, piece, rows, columns)
    out = jnp.zeros((count, blocks, 2, piece // 2, rows, columns), jnp.float32)
    split = orbitals.reshape((count,) + grid_shape)
    moved = []
    for index in range(count):
        parts = []
        for step in range(blocks):
            part = lax.dynamic_slice(
                split, (index, band ^ step, 0, 0, 0), (1, 1, piece, rows, columns)
            ).reshape(piece, rows, columns)
            if step:
                if index:
                    part = after(part, moved[index - 1][1])
                part = lax.ppermute(part, "band", [(at, at ^ step) for at in range(blocks)])
            parts.append(part)
        moved.append(parts)
    tables = (out, across, along, along_back, forth, back, weight)
    moved[1][0], out, across, along, along_back, forth, back, weight = lax.optimization_barrier(
        (moved[1][0],) + tables
    )

    def gather(index, shift, *earlier):
        parts = []
        for step in range(blocks):
            block = ((layer ^ step) + (blocks - shift)) % blocks
            part = lax.select_n(block ^ band, *moved[index])
            if earlier:
                part = after(part, *earlier)
            if step:
                part = lax.ppermute(part, "layer", [(at, at ^ step) for at in range(blocks)])
            parts.append(part)
        return parts

    known = {}
    for index in range(count):
        known[index] = gather(index, 0, *(known[index - 1][1:] if index else ()))

    def exchange(values):
        axes = ("inner", "band")
        return [
            lax.ppermute(value, axes, [(at, at ^ place % group) for at in range(group)])
            if place % group
            else value
            for place, value in enumerate(values)
        ]

    batches = batch_list(count)
    held, state = {}, {}
    previous = []

    def begin(step):
        order = int(step[1:])
        right = after(across, *previous)
        values = forward(batches[order], known, group, along, right)
        previous[:] = values[:1]
        state[step[1:]] = exchange(values)

    def middle(step):
        weights = after(weight, *previous)
        parts = 2 if step[1:] + "b" in ends else 1
        values = through_depth(state[step[1:]], planes, parts, forth, back, weights)
        previous[:] = values[:1]
        values = exchange(values)
        state[step[1:]], state[step[1:] + "b"] = values[:group], values[group:]

    def finish(step):
        order = int(step[1:].rstrip("b"))
        begin = planes // 2 if step.endswith("b") else 0
        right = after(across, *previous)
        uses = [[(i, j)] + ([(j, i)] if i != j < count else []) for i, j in batches[order]]
        results = inverse(state[step[1:]], uses, known, held, begin, along_back, right)
        previous[:] = [results[uses[0][0][0]]]
        if step[1:] + "b" in ends or step.endswith("b"):
            halves_of.append(results[count - 1])
        else:
            held.update(results)

    for index in range(count):
        known[count + index] = gather(index, 1, *known[count - 1][1:])
    steps = schedule(count)
    ends = {step[1:] for step in steps if step.endswith("b")}
    halves_of = []
    for step in steps:
        {"f": begin, "d": middle, "i": finish}[step[0]](step)

    everywhere = ("layer", "inner", "band")

    def route(step):
        spot = lambda at, within, along: (at * inner + within) * blocks + along
        return [
            (spot(q, i, b), spot(b ^ step, i, q))
            for q in range(blocks)
            for i in range(inner)
            for b in range(blocks)
        ]

    results = [(index, 0, held[index]) for index in range(count - 1)]
    results += [(count - 1, half, value) for half, value in enumerate(halves_of)]
    for index, half, result in results:
        result = result.reshape(-1, blocks, piece // 2, rows, columns)
        for step in range(blocks):
            part = lax.dynamic_index_in_dim(result, layer ^ band ^ step, 1, keepdims=False)
            part = lax.ppermute(part, everywhere, route(step))
            spot = (index, layer ^ step, half, 0, 0, 0)
            out = lax.dynamic_update_slice(out, part[None, None], spot)
    return out.reshape(count, planes, rows, columns)


def exchange_sum(value, split_axis, concat_axis):
    return lax.all_to_all(value, "slab", split_axis=split_axis, concat_axis=concat_axis, tiled=True)


def plain_body(orbitals):
    count, planes, rows, columns = orbitals.shape
    depth = planes * lax.axis_size("slab")
    blocks = lax.axis_size("band")
    pairs = [(source, (source + 1) % blocks) for source in range(blocks)]
    neighbour = lax.ppermute(orbitals, "band", pairs)
    x_count = jnp.arange(columns, dtype=jnp.int32)
    y_count = jnp.arange(rows, dtype=jnp.int32)
    z_count = jnp.arange(depth, dtype=jnp.int32)
    cas_x = cas_table(x_count, x_count, columns)
    cas_y = cas_table(y_count, y_count, rows)
    cas_z = cas_table(z_count, z_count, depth)
    slabs = lax.axis_size("slab")
    split_axis, extent = (2, rows) if rows % slabs == 0 else (3, columns)
    share = extent // slabs
    mine = lax.axis_index("slab") * share + jnp.arange(share, dtype=jnp.int32)
    y_rows, x_rows = (mine, x_count) if split_axis == 2 else (y_count, mine)
    squared = ((2.0 * math.pi / depth * frequency(z_count, depth)) ** 2)[:, None, None]
    squared = squared + ((2.0 * math.pi / rows * frequency(y_rows, rows)) ** 2)[None, :, None]
    squared = squared + ((2.0 * math.pi / columns * frequency(x_rows, columns)) ** 2)[None, None, :]
    weight = screened(squared) * (1.0 / (columns * rows * depth))
    result = jnp.zeros_like(orbitals)
    for partners in (orbitals, neighbour):
        density = (orbitals[:, None] * partners[None, :]).reshape((-1, planes, rows, columns))
        value = jnp.einsum("pzyx,xk->pzyk", density, cas_x, precision=highest)
        value = jnp.einsum("pzyx,yk->pzkx", value, cas_y, precision=highest)
        value = exchange_sum(value, split_axis, 1)
        value = jnp.einsum("pzyx,zk->pkyx", value, cas_z, precision=highest) * weight
        value = jnp.einsum("pzyx,zk->pkyx", value, cas_z, precision=highest)
        value = exchange_sum(value, 1, split_axis)
        value = jnp.einsum("pzyx,yk->pzkx", value, cas_y, precision=highest)
        value = jnp.einsum("pzyx,xk->pzyk", value, cas_x, precision=highest)
        field = value.reshape((count, count, planes, rows, columns))
        result = result - jnp.sum(field * partners[None], axis=1)
    return result


def solution(mesh):
    slabs, blocks = mesh.shape["slab"], mesh.shape["band"]

    def run(orbitals):
        planes = orbitals.shape[1] // slabs
        rows, columns = orbitals.shape[2:]
        inner = max(slabs // blocks, 1)
        share = rows // (inner * blocks)
        fits = slabs % blocks == 0 and planes % (4 * blocks) == 0 and planes % 16 == 0
        fits = fits and slabs & (slabs - 1) == 0 and blocks & (blocks - 1) == 0
        fits = fits and rows % (inner * blocks) == 0 and share % 8 == 0 and columns % 128 == 0
        if not fits:
            spec = P("band", "slab", None, None)
            return jax.shard_map(
                plain_body, mesh=mesh, in_specs=(spec,), out_specs=spec, check_vma=False
            )(orbitals)
        finer = Mesh(mesh.devices.reshape(blocks, inner, blocks), ("layer", "inner", "band"))
        spec = P("band", ("layer", "inner"), None, None)
        step = jax.shard_map(
            layered_body, mesh=finer, in_specs=(spec,), out_specs=spec, check_vma=False
        )
        return step(orbitals)

    return run
```

```python
import functools
import math

import jax
import jax.numpy as jnp
from jax import lax
from jax.experimental import pallas as pl
from jax.experimental.pallas import tpu as pltpu
from jax.sharding import Mesh, PartitionSpec as P


screen_width = 0.5
highest = lax.Precision.HIGHEST


def frequency(counter, length):
    return jnp.where(counter < length // 2, counter, counter - length).astype(jnp.float32)


def screened(squared):
    safe_sq = jnp.where(squared > 0, squared, 1.0)
    value = 4.0 * math.pi / safe_sq * (1.0 - jnp.exp(-safe_sq / (4.0 * screen_width**2)))
    return jnp.where(squared > 0, value, math.pi / screen_width**2)


def cas_table(rows, columns, length):
    product = rows[:, None] * columns[None, :] % length
    angles = 2.0 * math.pi / length * product.astype(jnp.float32)
    return jnp.cos(angles) + jnp.sin(angles)


def halves(value):
    high = value.astype(jnp.bfloat16)
    return high, (value - high.astype(jnp.float32)).astype(jnp.bfloat16)


def table_halves(table):
    high = lax.reduce_precision(table, exponent_bits=8, mantissa_bits=7)
    return high.astype(jnp.bfloat16), (table - high).astype(jnp.bfloat16)


def right_table(table):
    high, low = table_halves(table)
    top = jnp.concatenate([high, low], axis=1)
    return jnp.concatenate([top, jnp.concatenate([high, jnp.zeros_like(low)], axis=1)], axis=0)


def left_table(table):
    high, low = table_halves(table)
    top = jnp.concatenate([high, high], axis=1)
    return jnp.concatenate([top, jnp.concatenate([low, jnp.zeros_like(low)], axis=1)], axis=0)


def times_right(value, table):
    width = value.shape[1]
    high, low = halves(value)
    both = jnp.dot(
        jnp.concatenate([high, low], axis=1), table, preferred_element_type=jnp.float32
    )
    return both[:, :width] + both[:, width:]


def times_left(table, value):
    high, low = halves(value)
    both = jnp.dot(
        table, jnp.concatenate([high, low], axis=0), preferred_element_type=jnp.float32
    )
    rows = both.shape[0] // 2
    return both[:rows] + both[rows:]


def spot_of(plane, planes, pieces):
    half, reach = planes // 2, planes // pieces // 2
    return plane % half // reach, plane // half * reach + plane % reach


def pair_at(refs, lead, plane, planes, pieces):
    piece, place = spot_of(plane, planes, pieces)
    return refs[piece][lead, place : place + 2]


def forward_kernel(group, pieces, leads, pairs, left_ref, right_ref, *refs):
    refs, out_refs = refs[:-group], refs[-group:]
    _, piece, rows, columns = refs[0].shape
    share = rows // group
    planes = piece * pieces
    orbitals = [refs[at : at + pieces] for at in range(0, len(refs), pieces)]
    for which, (first, second) in enumerate(pairs):
        for plane in range(0, planes, 2):
            density = pair_at(orbitals[first], leads[first], plane, planes, pieces)
            density = density * pair_at(orbitals[second], leads[second], plane, planes, pieces)
            part = times_right(density.reshape(2 * rows, columns), right_ref[...])
            part = times_left(left_ref[...], jnp.concatenate([part[:rows], part[rows:]], axis=1))
            for offset in range(2):
                lines = part[:, offset * columns : (offset + 1) * columns]
                for chunk in range(group):
                    out_refs[chunk][which, pl.ds(plane + offset, share, stride=planes), :] = lines[
                        chunk * share : (chunk + 1) * share
                    ]


def depth_kernel(planes, group, forth_ref, back_ref, weight_ref, *refs):
    in_refs, out_refs = refs[:group], refs[group:]
    parts = len(out_refs) // group
    reach = planes // parts
    share = in_refs[0].shape[1] // planes
    columns = in_refs[0].shape[2]
    for row in range(0, share, 2):
        value = jnp.concatenate(
            [
                jnp.concatenate(
                    [ref[0, at * planes : (at + 1) * planes, :] for ref in in_refs], axis=0
                )
                for at in (row, row + 1)
            ],
            axis=1,
        )
        value = times_left(forth_ref[...], value) * weight_ref[row // 2]
        value = times_left(back_ref[...], value)
        for offset, at in enumerate((row, row + 1)):
            for place, ref in enumerate(out_refs):
                first = place % group * planes + place // group * reach
                ref[0, at * reach : (at + 1) * reach, :] = value[
                    first : first + reach, offset * columns : (offset + 1) * columns
                ]


def potential_planes(plane, planes, which, left_ref, right_ref, in_refs):
    columns = in_refs[0].shape[2]
    share = in_refs[0].shape[1] // planes
    rows = len(in_refs) * share
    value = jnp.concatenate(
        [
            jnp.concatenate(
                [ref[which, pl.ds(plane + offset, share, stride=planes), :] for ref in in_refs],
                axis=0,
            )
            for offset in range(2)
        ],
        axis=1,
    )
    value = times_left(left_ref[...], value)
    value = jnp.concatenate([value[:, :columns], value[:, columns:]], axis=0)
    return times_right(value, right_ref[...]).reshape(2, rows, columns)


def inverse_kernel(uses, names, pieces, group, begin, left_ref, right_ref, *refs):
    factors, leads, held, targets = names
    in_refs, refs = refs[:group], refs[group:]
    factor_refs = {
        factor: refs[place * pieces : (place + 1) * pieces] for place, factor in enumerate(factors)
    }
    planes = refs[0].shape[1] * pieces
    refs = refs[len(factors) * pieces :]
    held_refs, out_refs = dict(zip(held, refs)), dict(zip(targets, refs[len(held) :]))
    count = refs[-1].shape[0]
    for plane in range(0, count, 2):
        total = {target: held_refs[target][begin + plane : begin + plane + 2] for target in held}
        for which, pairs in enumerate(uses):
            field = potential_planes(plane, count, which, left_ref, right_ref, in_refs)
            for target, factor in pairs:
                spot = (leads[factor], begin + plane, planes, pieces)
                term = field * pair_at(factor_refs[factor], *spot)
                total[target] = total[target] - term if target in total else -term
        for target in targets:
            out_refs[target][plane : plane + 2] = total[target]


grant = pltpu.CompilerParams(vmem_limit_bytes=16 * 1024 * 1024)


def whole(shape):
    return pl.BlockSpec(shape, lambda *grid: (0,) * len(shape))


def cost(steps):
    return pl.CostEstimate(flops=steps * 700_000_000, bytes_accessed=steps * 3_000_000, transcendentals=0)


def forward(pairs, known, group, left, right):
    used = sorted({index for pair in pairs for index in pair})
    pieces = len(known[used[0]][0])
    _, piece, rows, columns = known[used[0]][0][0].shape
    leads = [known[index][1] for index in used]
    chunk = jax.ShapeDtypeStruct((len(pairs), rows // group * piece * pieces, columns), jnp.float32)
    places = [(used.index(first), used.index(second)) for first, second in pairs]
    return pl.pallas_call(
        functools.partial(forward_kernel, group, pieces, leads, places),
        out_shape=[chunk] * group,
        cost_estimate=cost(len(pairs)),
        compiler_params=grant,
        name="forward",
    )(left, right, *[part for index in used for part in known[index][0]])


def through_depth(values, planes, parts, forth, back, weight):
    count, lines, columns = values[0].shape
    group, reach = len(values), lines // parts

    def block(size):
        return pl.BlockSpec((1, size, columns), lambda step: (step, 0, 0))

    return pl.pallas_call(
        functools.partial(depth_kernel, planes, group),
        grid=(count,),
        in_specs=[whole(forth.shape), whole(back.shape), whole(weight.shape)]
        + [block(lines)] * group,
        out_specs=[block(reach)] * (group * parts),
        out_shape=[jax.ShapeDtypeStruct((count, reach, columns), jnp.float32)] * (group * parts),
        cost_estimate=cost(count),
        compiler_params=grant,
        name="through_depth",
    )(forth, back, weight, *values)


def inverse(values, uses, known, held, begin, left, right):
    factors = sorted({factor for pairs in uses for _, factor in pairs})
    targets = sorted({target for pairs in uses for target, _ in pairs})
    given = [target for target in targets if target in held]
    pieces = len(known[factors[0]][0])
    rows, columns = known[factors[0]][0][0].shape[2:]
    leads = {factor: known[factor][1] for factor in factors}
    planes = values[0].shape[1] * len(values) // rows
    result = jax.ShapeDtypeStruct((planes, rows, columns), jnp.float32)
    names = (factors, leads, given, targets)
    results = pl.pallas_call(
        functools.partial(inverse_kernel, uses, names, pieces, len(values), begin),
        out_shape=[result] * len(targets),
        cost_estimate=cost(len(uses)),
        compiler_params=grant,
        name="inverse",
    )(
        left,
        right,
        *values,
        *[part for factor in factors for part in known[factor][0]],
        *[held[target] for target in given],
    )
    return dict(zip(targets, results))


def batch_list(count):
    own = [[(i, j)] for j in range(count) for i in range(j + 1)]
    return own + [[(i, count + j)] for i in range(count) for j in range(count)]


def schedule(count):
    own, total = count * (count + 1) // 2, count * (count + 1) // 2 + count * count
    order = ["f0", "d0"] + [f"f{batch}" for batch in range(1, own)] + ["i0"]
    order += [f"d{batch}" for batch in range(1, own)]
    waiting = [f"i{batch}" for batch in range(1, own)]
    for batch in range(own, own + 2):
        order += [f"f{batch}"] + waiting[:1]
        waiting = waiting[1:]
    order += waiting + [f"d{own}"]
    for batch in range(own + 2, total):
        order += [f"f{batch}", f"d{batch - 1}", f"i{batch - 2}"]
    last = total - 1
    return order + [f"d{last}", f"i{last - 1}", f"i{last}", f"i{last}b"]


def after(value, *earlier):
    return lax.optimization_barrier((value,) + earlier)[0]


def layered_body(orbitals):
    blocks = lax.axis_size("band")
    inner = lax.axis_size("inner")
    count, planes, rows, columns = orbitals.shape
    piece = planes // blocks
    group = inner * blocks
    depth = planes * inner * blocks
    share = rows // group
    layer = lax.axis_index("layer")
    band = lax.axis_index("band")
    me = lax.axis_index(("inner", "band"))

    counter = jnp.arange(columns, dtype=jnp.int32)
    across = right_table(cas_table(counter, counter, columns))
    counter = jnp.arange(rows, dtype=jnp.int32)
    held_rows = (counter // share ^ me) * share + counter % share
    along_table = cas_table(held_rows, counter, rows)
    along = left_table(along_table)
    along_back = left_table(along_table.T)
    counter = jnp.arange(depth, dtype=jnp.int32)
    source, local = counter // planes ^ me, counter % planes
    slot, offset = spot_of(local, planes, blocks)
    place = (slot ^ layer) * (inner * planes) + source // blocks * planes
    place = place + source % blocks * piece + offset
    depth_table = cas_table(counter, place, depth)
    forth = left_table(depth_table)
    back = left_table(depth_table.T)

    freq_z = 2.0 * math.pi / depth * frequency(counter, depth)
    mine = me * share + jnp.arange(share, dtype=jnp.int32)
    freq_y = 2.0 * math.pi / rows * frequency(mine, rows)
    freq_x = 2.0 * math.pi / columns * frequency(jnp.arange(columns, dtype=jnp.int32), columns)
    squared = (freq_y**2).reshape(share // 2, 1, 2, 1) + (freq_z**2)[None, :, None, None]
    squared = squared + (freq_x**2)[None, None, None, :]
    weight = screened(squared) * (1.0 / (columns * rows * depth))
    weight = weight.reshape(share // 2, depth, 2 * columns)

    grid_shape = (blocks, piece, rows, columns)
    out = jnp.zeros((count, blocks, 2, piece // 2, rows, columns), jnp.float32)
    split = orbitals.reshape((count,) + grid_shape)
    moved = []
    for index in range(count):
        parts = []
        source = after(split, across) if index else split
        for step in range(blocks):
            part = lax.dynamic_slice(
                source, (index, band ^ step, 0, 0, 0), (1, 1, piece, rows, columns)
            ).reshape(piece, rows, columns)
            if step:
                if index:
                    part = after(part, moved[index - 1][1])
                part = lax.ppermute(part, "band", [(at, at ^ step) for at in range(blocks)])
            parts.append(part)
        moved.append(parts)
    tables = (out, across, along, along_back, forth, back, weight)
    moved[1][0], out, across, along, along_back, forth, back, weight = lax.optimization_barrier(
        (moved[1][0],) + tables
    )

    def gather(indices, shift, *earlier):
        parts = []
        for step in range(blocks):
            block = ((layer ^ step) + (blocks - shift)) % blocks
            part = jnp.stack([lax.select_n(block ^ band, *moved[index]) for index in indices])
            if earlier:
                part = after(part, *earlier)
            if step:
                part = lax.ppermute(part, "layer", [(at, at ^ step) for at in range(blocks)])
            parts.append(part)
        return parts

    known = {}
    for index in range(count):
        earlier = known[index - 1][0][1:] if index else ()
        known[index] = (gather([index], 0, *earlier), 0)

    def exchange(values):
        axes = ("inner", "band")
        return [
            lax.ppermute(value, axes, [(at, at ^ place % group) for at in range(group)])
            if place % group
            else value
            for place, value in enumerate(values)
        ]

    batches = batch_list(count)
    held, state = {}, {}
    previous = []

    def begin(step):
        order = int(step[1:])
        right = after(across, *previous)
        values = forward(batches[order], known, group, along, right)
        previous[:] = values[:1]
        state[step[1:]] = exchange(values)

    def middle(step):
        weights = after(weight, *previous)
        parts = 2 if step[1:] + "b" in ends else 1
        values = through_depth(state[step[1:]], planes, parts, forth, back, weights)
        previous[:] = values[:1]
        values = exchange(values)
        state[step[1:]], state[step[1:] + "b"] = values[:group], values[group:]

    def finish(step):
        order = int(step[1:].rstrip("b"))
        begin = planes // 2 if step.endswith("b") else 0
        right = after(across, *previous)
        uses = [[(i, j)] + ([(j, i)] if i != j < count else []) for i, j in batches[order]]
        results = inverse(state[step[1:]], uses, known, held, begin, along_back, right)
        previous[:] = [results[uses[0][0][0]]]
        if step[1:] + "b" in ends or step.endswith("b"):
            halves_of.append(results[count - 1])
        else:
            held.update(results)

    for index in range(count):
        earlier = () if index else known[count - 1][0][1:]
        known[count + index] = (gather([index], 1, *earlier), 0)
    steps = schedule(count)
    ends = {step[1:] for step in steps if step.endswith("b")}
    halves_of = []
    for step in steps:
        {"f": begin, "d": middle, "i": finish}[step[0]](step)

    everywhere = ("layer", "inner", "band")

    def route(step):
        spot = lambda at, within, along: (at * inner + within) * blocks + along
        return [
            (spot(q, i, b), spot(b ^ step, i, q))
            for q in range(blocks)
            for i in range(inner)
            for b in range(blocks)
        ]

    first_moved = []
    results = [(index, 0, held[index]) for index in range(count - 1)]
    results += [(count - 1, half, value) for half, value in enumerate(halves_of)]
    for index, half, result in results:
        result = result.reshape(-1, blocks, piece // 2, rows, columns)
        for step in range(blocks):
            part = lax.dynamic_index_in_dim(result, layer ^ band ^ step, 1, keepdims=False)
            if half:
                part = after(part, first_moved[step])
            part = lax.ppermute(part, everywhere, route(step))
            spot = (index, layer ^ step, half, 0, 0, 0)
            if not (index or half):
                first_moved.append(part)
            out = lax.dynamic_update_slice(out, part[None, None], spot)
    return out.reshape(count, planes, rows, columns)


def exchange_sum(value, split_axis, concat_axis):
    return lax.all_to_all(value, "slab", split_axis=split_axis, concat_axis=concat_axis, tiled=True)


def plain_body(orbitals):
    count, planes, rows, columns = orbitals.shape
    depth = planes * lax.axis_size("slab")
    blocks = lax.axis_size("band")
    pairs = [(source, (source + 1) % blocks) for source in range(blocks)]
    neighbour = lax.ppermute(orbitals, "band", pairs)
    x_count = jnp.arange(columns, dtype=jnp.int32)
    y_count = jnp.arange(rows, dtype=jnp.int32)
    z_count = jnp.arange(depth, dtype=jnp.int32)
    cas_x = cas_table(x_count, x_count, columns)
    cas_y = cas_table(y_count, y_count, rows)
    cas_z = cas_table(z_count, z_count, depth)
    slabs = lax.axis_size("slab")
    split_axis, extent = (2, rows) if rows % slabs == 0 else (3, columns)
    share = extent // slabs
    mine = lax.axis_index("slab") * share + jnp.arange(share, dtype=jnp.int32)
    y_rows, x_rows = (mine, x_count) if split_axis == 2 else (y_count, mine)
    squared = ((2.0 * math.pi / depth * frequency(z_count, depth)) ** 2)[:, None, None]
    squared = squared + ((2.0 * math.pi / rows * frequency(y_rows, rows)) ** 2)[None, :, None]
    squared = squared + ((2.0 * math.pi / columns * frequency(x_rows, columns)) ** 2)[None, None, :]
    weight = screened(squared) * (1.0 / (columns * rows * depth))
    result = jnp.zeros_like(orbitals)
    for partners in (orbitals, neighbour):
        density = (orbitals[:, None] * partners[None, :]).reshape((-1, planes, rows, columns))
        value = jnp.einsum("pzyx,xk->pzyk", density, cas_x, precision=highest)
        value = jnp.einsum("pzyx,yk->pzkx", value, cas_y, precision=highest)
        value = exchange_sum(value, split_axis, 1)
        value = jnp.einsum("pzyx,zk->pkyx", value, cas_z, precision=highest) * weight
        value = jnp.einsum("pzyx,zk->pkyx", value, cas_z, precision=highest)
        value = exchange_sum(value, 1, split_axis)
        value = jnp.einsum("pzyx,yk->pzkx", value, cas_y, precision=highest)
        value = jnp.einsum("pzyx,xk->pzyk", value, cas_x, precision=highest)
        field = value.reshape((count, count, planes, rows, columns))
        result = result - jnp.sum(field * partners[None], axis=1)
    return result


def solution(mesh):
    slabs, blocks = mesh.shape["slab"], mesh.shape["band"]

    def run(orbitals):
        planes = orbitals.shape[1] // slabs
        rows, columns = orbitals.shape[2:]
        inner = max(slabs // blocks, 1)
        share = rows // (inner * blocks)
        fits = slabs % blocks == 0 and planes % (4 * blocks) == 0 and planes % 16 == 0
        fits = fits and slabs & (slabs - 1) == 0 and blocks & (blocks - 1) == 0
        fits = fits and rows % (inner * blocks) == 0 and share % 8 == 0 and columns % 128 == 0
        if not fits:
            spec = P("band", "slab", None, None)
            return jax.shard_map(
                plain_body, mesh=mesh, in_specs=(spec,), out_specs=spec, check_vma=False
            )(orbitals)
        finer = Mesh(mesh.devices.reshape(blocks, inner, blocks), ("layer", "inner", "band"))
        spec = P("band", ("layer", "inner"), None, None)
        step = jax.shard_map(
            layered_body, mesh=finer, in_specs=(spec,), out_specs=spec, check_vma=False
        )
        return step(orbitals)

    return run
```

```python
import functools
import math

import jax
import jax.numpy as jnp
from jax import lax
from jax.experimental import pallas as pl
from jax.experimental.pallas import tpu as pltpu
from jax.sharding import Mesh, PartitionSpec as P


screen_width = 0.5
highest = lax.Precision.HIGHEST


def frequency(counter, length):
    return jnp.where(counter < length // 2, counter, counter - length).astype(jnp.float32)


def screened(squared):
    safe_sq = jnp.where(squared > 0, squared, 1.0)
    value = 4.0 * math.pi / safe_sq * (1.0 - jnp.exp(-safe_sq / (4.0 * screen_width**2)))
    return jnp.where(squared > 0, value, math.pi / screen_width**2)


def cas_table(rows, columns, length):
    product = rows[:, None] * columns[None, :] % length
    angles = 2.0 * math.pi / length * product.astype(jnp.float32)
    return jnp.cos(angles) + jnp.sin(angles)


def halves(value):
    high = value.astype(jnp.bfloat16)
    return high, (value - high.astype(jnp.float32)).astype(jnp.bfloat16)


def table_halves(table):
    high = lax.reduce_precision(table, exponent_bits=8, mantissa_bits=7)
    return high.astype(jnp.bfloat16), (table - high).astype(jnp.bfloat16)


def right_table(table):
    high, low = table_halves(table)
    top = jnp.concatenate([high, low], axis=1)
    return jnp.concatenate([top, jnp.concatenate([high, jnp.zeros_like(low)], axis=1)], axis=0)


def left_table(table):
    high, low = table_halves(table)
    top = jnp.concatenate([high, high], axis=1)
    return jnp.concatenate([top, jnp.concatenate([low, jnp.zeros_like(low)], axis=1)], axis=0)


def times_right(value, table):
    width = value.shape[1]
    high, low = halves(value)
    both = jnp.dot(
        jnp.concatenate([high, low], axis=1), table, preferred_element_type=jnp.float32
    )
    return both[:, :width] + both[:, width:]


def times_left(table, value):
    high, low = halves(value)
    both = jnp.dot(
        table, jnp.concatenate([high, low], axis=0), preferred_element_type=jnp.float32
    )
    rows = both.shape[0] // 2
    return both[:rows] + both[rows:]


def spot_of(plane, planes, pieces):
    half, reach = planes // 2, planes // pieces // 2
    return plane % half // reach, plane // half * reach + plane % reach


def pair_at(refs, lead, plane, planes, pieces):
    piece, place = spot_of(plane, planes, pieces)
    return refs[piece][lead, place : place + 2]


def forward_kernel(group, pieces, leads, pairs, left_ref, right_ref, *refs):
    refs, out_refs = refs[:-group], refs[-group:]
    _, piece, rows, columns = refs[0].shape
    share = rows // group
    planes = piece * pieces
    orbitals = [refs[at : at + pieces] for at in range(0, len(refs), pieces)]
    for which, (first, second) in enumerate(pairs):
        for plane in range(0, planes, 2):
            density = pair_at(orbitals[first], leads[first], plane, planes, pieces)
            density = density * pair_at(orbitals[second], leads[second], plane, planes, pieces)
            part = times_right(density.reshape(2 * rows, columns), right_ref[...])
            part = times_left(left_ref[...], jnp.concatenate([part[:rows], part[rows:]], axis=1))
            for offset in range(2):
                lines = part[:, offset * columns : (offset + 1) * columns]
                for chunk in range(group):
                    out_refs[chunk][which, pl.ds(plane + offset, share, stride=planes), :] = lines[
                        chunk * share : (chunk + 1) * share
                    ]


def depth_kernel(planes, group, forth_ref, back_ref, weight_ref, *refs):
    in_refs, out_refs = refs[:group], refs[group:]
    parts = len(out_refs) // group
    reach = planes // parts
    share = in_refs[0].shape[1] // planes
    columns = in_refs[0].shape[2]
    for row in range(0, share, 2):
        value = jnp.concatenate(
            [
                jnp.concatenate(
                    [ref[0, at * planes : (at + 1) * planes, :] for ref in in_refs], axis=0
                )
                for at in (row, row + 1)
            ],
            axis=1,
        )
        value = times_left(forth_ref[...], value) * weight_ref[row // 2]
        value = times_left(back_ref[...], value)
        for offset, at in enumerate((row, row + 1)):
            for place, ref in enumerate(out_refs):
                first = place % group * planes + place // group * reach
                ref[0, at * reach : (at + 1) * reach, :] = value[
                    first : first + reach, offset * columns : (offset + 1) * columns
                ]


def potential_planes(plane, planes, which, left_ref, right_ref, in_refs):
    columns = in_refs[0].shape[2]
    share = in_refs[0].shape[1] // planes
    rows = len(in_refs) * share
    value = jnp.concatenate(
        [
            jnp.concatenate(
                [ref[which, pl.ds(plane + offset, share, stride=planes), :] for ref in in_refs],
                axis=0,
            )
            for offset in range(2)
        ],
        axis=1,
    )
    value = times_left(left_ref[...], value)
    value = jnp.concatenate([value[:, :columns], value[:, columns:]], axis=0)
    return times_right(value, right_ref[...]).reshape(2, rows, columns)


def inverse_kernel(uses, names, pieces, group, begin, left_ref, right_ref, *refs):
    factors, leads, held, targets = names
    in_refs, refs = refs[:group], refs[group:]
    factor_refs = {
        factor: refs[place * pieces : (place + 1) * pieces] for place, factor in enumerate(factors)
    }
    planes = refs[0].shape[1] * pieces
    refs = refs[len(factors) * pieces :]
    held_refs, out_refs = dict(zip(held, refs)), dict(zip(targets, refs[len(held) :]))
    count = refs[-1].shape[0]
    for plane in range(0, count, 2):
        total = {target: held_refs[target][begin + plane : begin + plane + 2] for target in held}
        for which, pairs in enumerate(uses):
            field = potential_planes(plane, count, which, left_ref, right_ref, in_refs)
            for target, factor in pairs:
                spot = (leads[factor], begin + plane, planes, pieces)
                term = field * pair_at(factor_refs[factor], *spot)
                total[target] = total[target] - term if target in total else -term
        for target in targets:
            out_refs[target][plane : plane + 2] = total[target]


grant = pltpu.CompilerParams(vmem_limit_bytes=16 * 1024 * 1024)


def whole(shape):
    return pl.BlockSpec(shape, lambda *grid: (0,) * len(shape))


def cost(steps):
    return pl.CostEstimate(flops=steps * 700_000_000, bytes_accessed=steps * 3_000_000, transcendentals=0)


def forward(pairs, known, group, left, right):
    used = sorted({index for pair in pairs for index in pair})
    pieces = len(known[used[0]][0])
    _, piece, rows, columns = known[used[0]][0][0].shape
    leads = [known[index][1] for index in used]
    chunk = jax.ShapeDtypeStruct((len(pairs), rows // group * piece * pieces, columns), jnp.float32)
    places = [(used.index(first), used.index(second)) for first, second in pairs]
    return pl.pallas_call(
        functools.partial(forward_kernel, group, pieces, leads, places),
        out_shape=[chunk] * group,
        cost_estimate=cost(len(pairs)),
        compiler_params=grant,
        name="forward",
    )(left, right, *[part for index in used for part in known[index][0]])


def through_depth(values, planes, parts, forth, back, weight):
    count, lines, columns = values[0].shape
    group, reach = len(values), lines // parts

    def block(size):
        return pl.BlockSpec((1, size, columns), lambda step: (step, 0, 0))

    return pl.pallas_call(
        functools.partial(depth_kernel, planes, group),
        grid=(count,),
        in_specs=[whole(forth.shape), whole(back.shape), whole(weight.shape)]
        + [block(lines)] * group,
        out_specs=[block(reach)] * (group * parts),
        out_shape=[jax.ShapeDtypeStruct((count, reach, columns), jnp.float32)] * (group * parts),
        cost_estimate=cost(count),
        compiler_params=grant,
        name="through_depth",
    )(forth, back, weight, *values)


def inverse(values, uses, known, held, begin, left, right):
    factors = sorted({factor for pairs in uses for _, factor in pairs})
    targets = sorted({target for pairs in uses for target, _ in pairs})
    given = [target for target in targets if target in held]
    pieces = len(known[factors[0]][0])
    rows, columns = known[factors[0]][0][0].shape[2:]
    leads = {factor: known[factor][1] for factor in factors}
    planes = values[0].shape[1] * len(values) // rows
    result = jax.ShapeDtypeStruct((planes, rows, columns), jnp.float32)
    names = (factors, leads, given, targets)
    results = pl.pallas_call(
        functools.partial(inverse_kernel, uses, names, pieces, len(values), begin),
        out_shape=[result] * len(targets),
        cost_estimate=cost(len(uses)),
        compiler_params=grant,
        name="inverse",
    )(
        left,
        right,
        *values,
        *[part for factor in factors for part in known[factor][0]],
        *[held[target] for target in given],
    )
    return dict(zip(targets, results))


def batch_list(count):
    own = [[(i, j)] for j in range(count) for i in range(j + 1)]
    return own + [[(i, count + j)] for i in range(count) for j in range(count)]


def schedule(count):
    own, total = count * (count + 1) // 2, count * (count + 1) // 2 + count * count
    order = ["f0", "d0"] + [f"f{batch}" for batch in range(1, own)] + ["i0"]
    order += [f"d{batch}" for batch in range(1, own)]
    waiting = [f"i{batch}" for batch in range(1, own)]
    for batch in range(own, own + 2):
        order += [f"f{batch}"] + waiting[:1]
        waiting = waiting[1:]
    order += waiting + [f"d{own}"]
    for batch in range(own + 2, total):
        order += [f"f{batch}", f"d{batch - 1}", f"i{batch - 2}"]
    last = total - 1
    return order + [f"d{last}", f"i{last - 1}", f"i{last}", f"i{last}b"]


def after(value, *earlier):
    return lax.optimization_barrier((value,) + earlier)[0]


def layered_body(orbitals):
    blocks = lax.axis_size("band")
    inner = lax.axis_size("inner")
    count, planes, rows, columns = orbitals.shape
    piece = planes // blocks
    group = inner * blocks
    depth = planes * inner * blocks
    share = rows // group
    layer = lax.axis_index("layer")
    band = lax.axis_index("band")
    me = lax.axis_index(("inner", "band"))

    counter = jnp.arange(columns, dtype=jnp.int32)
    across = right_table(cas_table(counter, counter, columns))
    counter = jnp.arange(rows, dtype=jnp.int32)
    held_rows = (counter // share ^ me) * share + counter % share
    along_table = cas_table(held_rows, counter, rows)
    along = left_table(along_table)
    along_back = left_table(along_table.T)
    counter = jnp.arange(depth, dtype=jnp.int32)
    source, local = counter // planes ^ me, counter % planes
    slot, offset = spot_of(local, planes, blocks)
    place = (slot ^ layer) * (inner * planes) + source // blocks * planes
    place = place + source % blocks * piece + offset
    depth_table = cas_table(counter, place, depth)
    forth = left_table(depth_table)
    back = left_table(depth_table.T)

    freq_z = 2.0 * math.pi / depth * frequency(counter, depth)
    mine = me * share + jnp.arange(share, dtype=jnp.int32)
    freq_y = 2.0 * math.pi / rows * frequency(mine, rows)
    freq_x = 2.0 * math.pi / columns * frequency(jnp.arange(columns, dtype=jnp.int32), columns)
    squared = (freq_y**2).reshape(share // 2, 1, 2, 1) + (freq_z**2)[None, :, None, None]
    squared = squared + (freq_x**2)[None, None, None, :]
    weight = screened(squared) * (1.0 / (columns * rows * depth))
    weight = weight.reshape(share // 2, depth, 2 * columns)

    grid_shape = (blocks, piece, rows, columns)
    out = jnp.zeros((count, blocks, 2, piece // 2, rows, columns), jnp.float32)
    split = orbitals.reshape((count,) + grid_shape)
    moved = []
    for index in range(count):
        parts = []
        source = after(split, across) if index else split
        for step in range(blocks):
            part = lax.dynamic_slice(
                source if step else after(split, across), (index, band ^ step, 0, 0, 0), (1, 1, piece, rows, columns)
            ).reshape(piece, rows, columns)
            if step:
                if index:
                    part = after(part, moved[index - 1][1])
                part = lax.ppermute(part, "band", [(at, at ^ step) for at in range(blocks)])
            parts.append(part)
        moved.append(parts)
    tables = (out, across, along, along_back, forth, back, weight)
    moved[1][0], out, across, along, along_back, forth, back, weight = lax.optimization_barrier(
        (moved[1][0],) + tables
    )

    def gather(indices, shift, *earlier):
        parts = []
        sources = {index: moved[index] for index in indices}
        if shift:
            sources = {index: lax.optimization_barrier((moved[index], known[0][0][1]))[0] for index in indices}
        for step in range(blocks):
            block = ((layer ^ step) + (blocks - shift)) % blocks
            part = jnp.stack([lax.select_n(block ^ band, *sources[index]) for index in indices])
            if earlier and step:
                part = after(part, *earlier)
            if step:
                part = lax.ppermute(part, "layer", [(at, at ^ step) for at in range(blocks)])
            parts.append(part)
        return parts

    known = {}
    for index in range(count):
        earlier = known[index - 1][0][1:] if index else ()
        known[index] = (gather([index], 0, *earlier), 0)

    def exchange(values):
        moved = []
        for place, value in enumerate(values):
            step = place % group
            if step:
                pairs = [(at, at ^ step) for at in range(group)]
                value = lax.ppermute(value, ("inner", "band"), pairs)
            moved.append(value)
        return moved

    batches = batch_list(count)
    held, state = {}, {}
    previous = []

    def begin(step):
        order = int(step[1:])
        right = after(across, *previous)
        values = forward(batches[order], known, group, along, right)
        previous[:] = values[:1]
        state[step[1:]] = exchange(values)

    def middle(step):
        weights = after(weight, *previous)
        parts = 2 if step[1:] + "b" in ends else 1
        values = through_depth(state[step[1:]], planes, parts, forth, back, weights)
        previous[:] = values[:1]
        values = exchange(values)
        state[step[1:]], state[step[1:] + "b"] = values[:group], values[group:]

    def finish(step):
        order = int(step[1:].rstrip("b"))
        begin = planes // 2 if step.endswith("b") else 0
        right = after(across, *previous)
        uses = [[(i, j)] + ([(j, i)] if i != j < count else []) for i, j in batches[order]]
        results = inverse(state[step[1:]], uses, known, held, begin, along_back, right)
        previous[:] = [results[uses[0][0][0]]]
        if step[1:] + "b" in ends or step.endswith("b"):
            halves_of.append(results[count - 1])
        else:
            held.update(results)

    for index in range(count):
        earlier = () if index else known[count - 1][0][1:]
        known[count + index] = (gather([index], 1, *earlier), 0)
    steps = schedule(count)
    ends = {step[1:] for step in steps if step.endswith("b")}
    halves_of = []
    for step in steps:
        {"f": begin, "d": middle, "i": finish}[step[0]](step)

    everywhere = ("layer", "inner", "band")

    def route(step):
        spot = lambda at, within, along: (at * inner + within) * blocks + along
        return [
            (spot(q, i, b), spot(b ^ step, i, q))
            for q in range(blocks)
            for i in range(inner)
            for b in range(blocks)
        ]

    first_moved = []
    results = [(index, 0, held[index]) for index in range(count - 1)]
    results += [(count - 1, half, value) for half, value in enumerate(halves_of)]
    for index, half, result in results:
        result = result.reshape(-1, blocks, piece // 2, rows, columns)
        for step in range(blocks):
            part = lax.dynamic_index_in_dim(result, layer ^ band ^ step, 1, keepdims=False)
            if half:
                part = after(part, first_moved[step])
            part = lax.ppermute(part, everywhere, route(step))
            spot = (index, layer ^ step, half, 0, 0, 0)
            if not (index or half):
                first_moved.append(part)
            out = lax.dynamic_update_slice(out, part[None, None], spot)
    return out.reshape(count, planes, rows, columns)


def exchange_sum(value, split_axis, concat_axis):
    return lax.all_to_all(value, "slab", split_axis=split_axis, concat_axis=concat_axis, tiled=True)


def plain_body(orbitals):
    count, planes, rows, columns = orbitals.shape
    depth = planes * lax.axis_size("slab")
    blocks = lax.axis_size("band")
    pairs = [(source, (source + 1) % blocks) for source in range(blocks)]
    neighbour = lax.ppermute(orbitals, "band", pairs)
    x_count = jnp.arange(columns, dtype=jnp.int32)
    y_count = jnp.arange(rows, dtype=jnp.int32)
    z_count = jnp.arange(depth, dtype=jnp.int32)
    cas_x = cas_table(x_count, x_count, columns)
    cas_y = cas_table(y_count, y_count, rows)
    cas_z = cas_table(z_count, z_count, depth)
    slabs = lax.axis_size("slab")
    split_axis, extent = (2, rows) if rows % slabs == 0 else (3, columns)
    share = extent // slabs
    mine = lax.axis_index("slab") * share + jnp.arange(share, dtype=jnp.int32)
    y_rows, x_rows = (mine, x_count) if split_axis == 2 else (y_count, mine)
    squared = ((2.0 * math.pi / depth * frequency(z_count, depth)) ** 2)[:, None, None]
    squared = squared + ((2.0 * math.pi / rows * frequency(y_rows, rows)) ** 2)[None, :, None]
    squared = squared + ((2.0 * math.pi / columns * frequency(x_rows, columns)) ** 2)[None, None, :]
    weight = screened(squared) * (1.0 / (columns * rows * depth))
    result = jnp.zeros_like(orbitals)
    for partners in (orbitals, neighbour):
        density = (orbitals[:, None] * partners[None, :]).reshape((-1, planes, rows, columns))
        value = jnp.einsum("pzyx,xk->pzyk", density, cas_x, precision=highest)
        value = jnp.einsum("pzyx,yk->pzkx", value, cas_y, precision=highest)
        value = exchange_sum(value, split_axis, 1)
        value = jnp.einsum("pzyx,zk->pkyx", value, cas_z, precision=highest) * weight
        value = jnp.einsum("pzyx,zk->pkyx", value, cas_z, precision=highest)
        value = exchange_sum(value, 1, split_axis)
        value = jnp.einsum("pzyx,yk->pzkx", value, cas_y, precision=highest)
        value = jnp.einsum("pzyx,xk->pzyk", value, cas_x, precision=highest)
        field = value.reshape((count, count, planes, rows, columns))
        result = result - jnp.sum(field * partners[None], axis=1)
    return result


def solution(mesh):
    slabs, blocks = mesh.shape["slab"], mesh.shape["band"]

    def run(orbitals):
        planes = orbitals.shape[1] // slabs
        rows, columns = orbitals.shape[2:]
        inner = max(slabs // blocks, 1)
        share = rows // (inner * blocks)
        fits = slabs % blocks == 0 and planes % (4 * blocks) == 0 and planes % 16 == 0
        fits = fits and slabs & (slabs - 1) == 0 and blocks & (blocks - 1) == 0
        fits = fits and rows % (inner * blocks) == 0 and share % 8 == 0 and columns % 128 == 0
        if not fits:
            spec = P("band", "slab", None, None)
            return jax.shard_map(
                plain_body, mesh=mesh, in_specs=(spec,), out_specs=spec, check_vma=False
            )(orbitals)
        finer = Mesh(mesh.devices.reshape(blocks, inner, blocks), ("layer", "inner", "band"))
        spec = P("band", ("layer", "inner"), None, None)
        step = jax.shard_map(
            layered_body, mesh=finer, in_specs=(spec,), out_specs=spec, check_vma=False
        )
        return step(orbitals)

    return run
```
